256 devices in a mesh: grp: 8 (over z_hi, core), dev: 32 (over z_lo, y, x).
Axes of the slice: x: 4, y: 4, z: 8 (z_hi: 4, z_lo: 2; z = z_hi * 2 + z_lo), core: 2. Of those that a mesh axis runs over, the one named last changes fastest.
Arguments:
- user_factors: float32 [32768, 256], P(('grp', 'dev')), may hold values from -0.5 to 0.5
- item_factors: float32 [16384, 256], P(('grp', 'dev')), may hold values from -0.5 to 0.5
- user_items: int32 [32768, 8, 3], P(('grp', 'dev')), may hold values from 0 to 2047, as said below
- user_conf: float32 [32768, 8, 3], P(('grp', 'dev')), may hold values from 1 to 200
- user_mask: int32 [32768, 8, 3], P(('grp', 'dev')), may hold values 0 or 1
- item_users: int32 [16384, 8, 6], P(('grp', 'dev')), may hold values from 0 to 4095, as said below
- item_conf: float32 [16384, 8, 6], P(('grp', 'dev')), may hold values from 1 to 200
- item_mask: int32 [16384, 8, 6], P(('grp', 'dev')), may hold values 0 or 1
Outputs:
- new_users: float32 [32768, 256], P(('grp', 'dev'))
- new_items: float32 [16384, 256], P(('grp', 'dev'))
The draws below stay inside these ranges and needn't reach their ends.
Inputs may be any that keep to these rules, and one draw needn't show every extreme that they name: Within owner block c, id // 64 is the owner device and id % 64 its row. The user_items of the users of one device, in one owner block, name at most 16 distinct rows of any one owner device, and in every block each device names exactly 16 distinct rows of some owner device. Within owner block c, id // 128 is the owner device and id % 128 its row. The item_users of the items of one device, in one owner block, name at most 16 distinct rows of any one owner device, and in every block each device names exactly 16 distinct rows of some owner device.
All inputs are finite; a program needn't handle non-finite values. No bound on the sum of `user_mask` or of `item_mask` on one device may be relied on, other than what follows from the above.
Results may differ from the reference program's by a relative error of at most 0.0044.
Values may be sent and summed in bfloat16 or wider, within the bound.
A program may use at most 128 MiB of HBM per device.

```python
import math
import jax
import jax.numpy as jnp
from jax import lax

RANK = 256
USERS_DEV = 128
ITEMS_DEV = 64
USER_SLOTS = 3
ITEM_SLOTS = 6
REQUESTS = 16
CG_STEPS = 4
USERS = 32768
ITEMS = 16384
N_GRP = 8
N_DEV = 32


def draw_named_rows(key, total_rows, per_device, owner_rows, slots):
    keys = jax.random.split(key, 4)
    devices = total_rows // per_device
    owner = jax.random.randint(keys[0], (total_rows, N_GRP, slots), 0, N_DEV, dtype=jnp.int32)
    pick = jax.random.randint(keys[1], (total_rows, N_GRP, slots), 0, REQUESTS, dtype=jnp.int32)
    offset = jax.random.randint(keys[2], (devices, N_GRP, N_DEV), 0, owner_rows, dtype=jnp.int32)
    favored = jax.random.randint(keys[3], (devices, N_GRP), 0, N_DEV, dtype=jnp.int32)
    row_index = jnp.arange(total_rows, dtype=jnp.int32)
    device_of = (row_index // per_device).astype(jnp.int32)
    position = ((row_index % per_device)[:, None, None] * slots + jnp.arange(slots, dtype=jnp.int32)[None, None, :]).astype(jnp.int32)
    position = jnp.broadcast_to(position, (total_rows, N_GRP, slots))
    chosen = jnp.broadcast_to(favored[device_of][:, :, None], (total_rows, N_GRP, slots))
    early = position < REQUESTS
    owner = jnp.where(early, chosen, owner)
    pick = jnp.where(early, position, pick)
    block_index = jnp.broadcast_to(jnp.arange(N_GRP, dtype=jnp.int32)[None, :, None], (total_rows, N_GRP, slots))
    device_full = jnp.broadcast_to(device_of[:, None, None], (total_rows, N_GRP, slots))
    start = offset[device_full, block_index, owner]
    return (owner * owner_rows + (start + pick) % owner_rows).astype(jnp.int32)


def draw_user_items(key, part):
    return draw_named_rows(jax.random.fold_in(key, 11), USERS, USERS_DEV, ITEMS_DEV, USER_SLOTS)


def draw_item_users(key, part):
    return draw_named_rows(jax.random.fold_in(key, 23), ITEMS, ITEMS_DEV, USERS_DEV, ITEM_SLOTS)


def plant(result, key, low, largest):
    longest = result.shape.index(max(result.shape))
    spots = []
    for shift in (0, 1):
        where = [jax.random.randint(jax.random.fold_in(key, axis), (), 0, length) for axis, length in enumerate(result.shape)]
        where[longest] = (where[longest] + shift) % result.shape[longest]
        spots.append(tuple(where))
    return result.at[spots[0]].set(low).at[spots[1]].set(largest)


def block_scale(rng, dims, pieces, smallest, top_value):
    level, own = 1.0, jax.random.fold_in(rng, 6)
    for dim, parts in pieces:
        heights = jnp.exp(jax.random.uniform(jax.random.fold_in(own, dim), (parts,), jnp.float32, smallest / len(pieces), top_value / len(pieces)))
        level = level * jnp.repeat(heights, dims[dim] // parts).reshape([-1 if axis == dim else 1 for axis in range(len(dims))])
    return level


def centred(rng, shape, width, most, shards=(), kind=jnp.bfloat16):
    result = width * jax.random.normal(rng, shape, jnp.float32)
    if shards:
        result = result * block_scale(rng, shape, shards, -0.22, 0.18)
    return jnp.clip(result, -most, most).astype(kind)


def setup_inputs(seed: int = 0) -> dict:
    arg_keys = jax.random.split(jax.random.key(seed), 9)
    user_factors = centred(arg_keys[0], (USERS, RANK), 0.0625, 0.5, ((0, 256),), jnp.float32)
    item_factors = centred(arg_keys[1], (ITEMS, RANK), 0.0625, 0.5, ((0, 256),), jnp.float32)
    user_items = draw_user_items(jax.random.fold_in(arg_keys[8], 71), 0)
    user_conf = jnp.clip(jnp.exp(math.log(200.0) - 5.2983174 * jax.random.uniform(arg_keys[3], (USERS, N_GRP, USER_SLOTS), jnp.float32) ** block_scale(arg_keys[3], (USERS, N_GRP, USER_SLOTS), ((0, 256),), -0.2, 0.2)), 1.0, 200.0)
    user_mask = plant((jax.random.randint(arg_keys[4], (USERS, N_GRP, USER_SLOTS), 0, 4) < 3).astype(jnp.int32), jax.random.fold_in(arg_keys[4], 1), 0, 1)
    item_users = draw_item_users(jax.random.fold_in(arg_keys[8], 71), 0)
    item_conf = jnp.clip(jnp.exp(math.log(200.0) - 5.2983174 * jax.random.uniform(arg_keys[6], (ITEMS, N_GRP, ITEM_SLOTS), jnp.float32) ** block_scale(arg_keys[6], (ITEMS, N_GRP, ITEM_SLOTS), ((0, 256),), -0.2, 0.2)), 1.0, 200.0)
    item_mask = plant((jax.random.randint(arg_keys[7], (ITEMS, N_GRP, ITEM_SLOTS), 0, 4) < 3).astype(jnp.int32), jax.random.fold_in(arg_keys[7], 1), 0, 1)
    return {"user_factors": user_factors, "item_factors": item_factors, "user_items": user_items, "user_conf": user_conf, "user_mask": user_mask, "item_users": item_users, "item_conf": item_conf, "item_mask": item_mask}


ridge = 1.0


def solve_rows(gram, start_x, rows, confidence, slot_mask):
    maskf = slot_mask.astype(jnp.float32)
    weight = confidence * maskf
    rhs = jnp.einsum('us,usr->ur', maskf * (1.0 + confidence), rows, precision=lax.Precision.HIGHEST)

    def apply(vector):
        along = jnp.einsum('usr,ur->us', rows, vector, precision=lax.Precision.HIGHEST)
        extra = jnp.einsum('us,usr->ur', weight * along, rows, precision=lax.Precision.HIGHEST)
        return jnp.dot(vector, gram, precision=lax.Precision.HIGHEST) + ridge * vector + extra

    solution = start_x
    resid = rhs - apply(solution)
    direction = resid
    norm_now = jnp.sum(resid * resid, axis=1, keepdims=True)
    for step in range(CG_STEPS):
        image = apply(direction)
        alpha = norm_now / jnp.sum(direction * image, axis=1, keepdims=True)
        solution = solution + alpha * direction
        resid = resid - alpha * image
        norm_next = jnp.sum(resid * resid, axis=1, keepdims=True)
        direction = resid + (norm_next / norm_now) * direction
        norm_now = norm_next
    return solution


def half_step(start_x, other, slot_ids, confidence, slot_mask):
    packed = other.astype(jnp.bfloat16)
    gram = lax.dot_general(packed, packed, (((0,), (0,)), ((), ())), preferred_element_type=jnp.float32)
    block_rows = other.shape[0] // N_GRP
    total = start_x.shape[0]
    per_block = total // (N_GRP * N_DEV)
    offsets = (jnp.arange(N_GRP, dtype=jnp.int32) * block_rows).astype(jnp.int32)
    slots = slot_ids.shape[2]

    def one_block(operands):
        block_x, block_ids, block_conf, block_mask = operands
        index = (block_ids + offsets[None, :, None]).astype(jnp.int32)
        rows = packed[index].astype(jnp.float32) * block_mask[..., None].astype(jnp.float32)
        rows = rows.reshape(per_block, N_GRP * slots, -1)
        return solve_rows(gram, block_x, rows, block_conf.reshape(per_block, -1), block_mask.reshape(per_block, -1))

    shaped = (start_x.reshape(N_GRP * N_DEV, per_block, -1),
              slot_ids.reshape(N_GRP * N_DEV, per_block, N_GRP, slots),
              confidence.reshape(N_GRP * N_DEV, per_block, N_GRP, slots),
              slot_mask.reshape(N_GRP * N_DEV, per_block, N_GRP, slots))
    return lax.map(one_block, shaped).reshape(total, -1)


def reference(user_factors, item_factors, user_items, user_conf, user_mask, item_users, item_conf, item_mask):
    new_users = half_step(user_factors, item_factors, user_items, user_conf, user_mask)
    new_items = half_step(item_factors, new_users, item_users, item_conf, item_mask)
    return new_users, new_items
```

```python
import functools

import jax
import jax.numpy as jnp
from jax import lax
from jax.experimental import pallas as pl
from jax.experimental.pallas import tpu as pltpu
from jax.sharding import PartitionSpec as P

MESH = pl.DeviceIdType.MESH
CG_STEPS = 4
RANK = 256
NX, NY, NZ = 4, 4, 8
SIZES = {"x": NX, "y": NY, "z": NZ}
ORDERS = (("z", "y", "x"), ("z", "x", "y"), ("x", "y", "z"))


def units_of(rows):
    units = rows // 16 * 2
    last = units // 4
    side = (units - last) // 2
    return (side, side, last)


def buffer_shape(order, units):
    return (2,) + tuple(SIZES[a] for a in order[::-1]) + (units, 16, 128)


def my_coords():
    grp, dev = lax.axis_index("grp"), lax.axis_index("dev")
    core = grp % 2
    z = grp // 2 * 2 + dev // 16
    return {"core": core, "z": z, "y": dev // 4 % 4, "x": dev % 4}


def device_at(coords):
    return {
        "grp": coords["z"] // 2 * 2 + coords["core"],
        "dev": coords["z"] % 2 * 16 + coords["y"] * 4 + coords["x"],
    }


def neighbour(me, axis, shift):
    there = dict(me)
    size = SIZES[axis]
    there[axis] = (me[axis] + shift + size) % size
    return device_at(there)


def gather_kernel(*refs):
    ins, outs = refs[:3], refs[3:6]
    send_sem, recv_sem, local_sem = refs[6:]
    me = my_coords()
    core = me["core"]
    partner = device_at({**me, "core": 1 - core})

    barrier = pltpu.get_barrier_semaphore()
    around = [partner] + [neighbour(me, a, s) for a in "xyz" for s in (1, -1)]
    for other in around:
        pl.semaphore_signal(barrier, inc=1, device_id=other, device_id_type=MESH)
    pl.semaphore_wait(barrier, len(around))

    issued = []
    hand_overs = []
    counter = [0]

    def remote(src, dst, target):
        e = counter[0]
        counter[0] += 1
        copy = pltpu.make_async_remote_copy(
            src_ref=src,
            dst_ref=dst,
            send_sem=send_sem.at[e],
            recv_sem=recv_sem.at[e],
            device_id=target,
            device_id_type=MESH,
        )
        copy.start()
        issued.append(copy)
        return copy

    def block(colour, phase, v, half=None):
        order = ORDERS[colour]
        ref = outs[colour]
        index = [core] + [me[order[k]] for k in range(2, phase, -1)] + [v]
        if half is not None:
            inner = ref.shape[len(index)]
            cut = inner // 2
            index.append(pl.ds(0, cut) if half == 0 else pl.ds(cut, inner - cut))
        return ref.at[tuple(index)]

    steps = []
    for colour, order in enumerate(ORDERS):
        steps.append([(ph, k) for ph in range(3) for k in range(SIZES[order[ph]] // 2)])
    local = []
    for colour in range(3):
        own = outs[colour].at[(core,) + tuple(me[a] for a in ORDERS[colour][::-1])]
        copy = pltpu.make_async_copy(ins[colour], own, local_sem.at[colour])
        copy.start()
        local.append(copy)

    flying = [None] * 3

    def send(colour, phase, k):
        axis = ORDERS[colour][phase]
        size = SIZES[axis]
        last = k == size // 2 - 1
        pair = []
        for way in (0, 1):
            shift = 1 if way == 0 else -1
            v = (me[axis] - shift * k + size) % size
            half = way if last and size > 2 else None
            dst = block(colour, phase, v, half)
            src = dst
            if phase == 0 and k == 0:
                src = ins[colour]
            pair.append(remote(src, dst, neighbour(me, axis, shift)))
        flying[colour] = (phase, k, pair)

    def arrived(colour, way):
        phase, k, pair = flying[colour]
        pair[way].wait_recv()
        if phase == 2:
            axis = ORDERS[colour][phase]
            size = SIZES[axis]
            shift = 1 if way == 0 else -1
            v = (me[axis] - shift * (k + 1) + 2 * size) % size
            half = way if k == size // 2 - 1 else None
            got = block(colour, phase, v, half)
            hand_overs.append(remote(got, got, partner))

    for r in range(max(len(s) for s in steps) + 1):
        for colour in range(3):
            if r > len(steps[colour]):
                continue
            if r > 0:
                for way in (0, 1):
                    arrived(colour, way)
            if r == len(steps[colour]):
                continue
            phase, k = steps[colour][r]
            if phase == 1 and k == 0:
                local[colour].wait()
            if phase == 2 and k == 0:
                slab = block(colour, 2, me[ORDERS[colour][2]])
                hand_overs.append(remote(slab, slab, partner))
            send(colour, phase, k)
    for copy in hand_overs:
        copy.wait_recv()
    for copy in issued:
        copy.wait_send()


def copies_of():
    total = 0
    for order in ORDERS:
        total += 2 * sum(SIZES[a] // 2 for a in order)
        total += 1 + 2 * (SIZES[order[2]] // 2)
    return total


def gather_table(pieces, collective_id):
    copies = copies_of()
    units = [p.shape[0] for p in pieces]
    return pl.pallas_call(
        gather_kernel,
        out_shape=[
            jax.ShapeDtypeStruct(buffer_shape(o, u), jnp.bfloat16) for o, u in zip(ORDERS, units)
        ],
        in_specs=[pl.BlockSpec(memory_space=pltpu.VMEM)] * 3,
        out_specs=[pl.BlockSpec(memory_space=pl.ANY)] * 3,
        scratch_shapes=[
            pltpu.SemaphoreType.DMA((copies,)),
            pltpu.SemaphoreType.DMA((copies,)),
            pltpu.SemaphoreType.DMA((3,)),
        ],
        compiler_params=pltpu.CompilerParams(collective_id=collective_id, has_side_effects=True),
        name=f"gather_table_{collective_id}",
    )(*pieces)


def split_two(value):
    high = value.astype(jnp.bfloat16)
    low = (value - high.astype(jnp.float32)).astype(jnp.bfloat16)
    return jnp.concatenate([high, low], axis=0)


def dot(a, b):
    return jnp.dot(a, b, preferred_element_type=jnp.float32)


def solve_kernel(n, owner_rows, units, pack, *refs):
    tables = refs[:3]
    code_ref, weight_ref, gain_ref, start_ref = refs[3:7]
    out_ref = refs[7]
    packed = refs[8:11] if pack else ()
    scratch = refs[8 + len(packed):]
    (both, flipped, picked_t, picked, gram, gram2, diag, x_s, r_s, p_s) = scratch
    g = pl.program_id(0)
    slots = code_ref.shape[1]
    groups = owner_rows // 16
    total = slots * 8

    def tile(zl, y, x, j):
        if j < units[0]:
            return tables[0][0, x, y, zl, j]
        j -= units[0]
        if j < units[1]:
            return tables[1][0, y, x, zl, j]
        return tables[2][0, zl, y, x, j - units[1]]

    code = code_ref[pl.ds(g, 1), :]
    for chunk in range(2 * groups):
        zl, group = divmod(chunk, groups)
        span = pl.ds(chunk * 256, 256)
        halves = []
        for h in (0, 1):
            parts = [tile(zl, y, x, 2 * group + h) for y in range(NY) for x in range(NX)]
            halves.append(jnp.concatenate(parts, axis=0))
        rows = jnp.concatenate(halves, axis=1)
        both[span, 0:256] = rows
        flipped[:, span] = rows.T
        position = lax.broadcasted_iota(jnp.int32, (256, slots), 0) + chunk * 256
        both[span, 256 : 256 + slots] = jnp.where(position == code, 1.0, 0.0).astype(jnp.bfloat16)
    product = dot(flipped[...], both[...])

    @pl.when(g == 0)
    def _():
        gram[...] = product[:, 0:256]

    @pl.when(g > 0)
    def _():
        gram[...] += product[:, 0:256]

    here = product[:, 256 : 256 + slots]
    lanes = pl.ds(pl.multiple_of(g * slots, 128), slots)
    picked_t[:, lanes] = here.astype(jnp.bfloat16)
    picked[pl.ds(pl.multiple_of(g * slots, 128), slots), :] = here.T.astype(jnp.bfloat16)
    lane = lax.broadcasted_iota(jnp.int32, (n, slots), 1)
    own = lane % n == lax.broadcasted_iota(jnp.int32, (n, slots), 0)
    diag[:, lanes] = jnp.where(own, weight_ref[pl.ds(g, 1), :], 0.0)

    @pl.when(g == 7)
    def _():
        whole = gram[...]
        high = whole.astype(jnp.bfloat16)
        gram2[:, 0:256] = high
        gram2[:, 256:512] = (whole - high.astype(jnp.float32)).astype(jnp.bfloat16)
        width = 768

        def apply(vector):
            two = split_two(vector)
            by_gram = dot(two, gram2[...])
            image = by_gram[:n, :256] + by_gram[:n, 256:] + by_gram[n:, :256] + vector
            extra = jnp.zeros((2 * n, RANK), jnp.float32)
            for at in range(0, total, width):
                along = dot(two, picked_t[:, at : at + width])
                along = (along[:n] + along[n:]) * diag[:, at : at + width]
                extra = extra + dot(split_two(along), picked[at : at + width, :])
            return image + extra[:n] + extra[n:]

        rhs = jnp.zeros((2 * n, RANK), jnp.float32)
        for block in range(8):
            gains = jnp.where(own, gain_ref[block : block + 1, :], 0.0)
            rhs = rhs + dot(split_two(gains), picked[block * slots : (block + 1) * slots, :])
        start = start_ref[...]
        resid = rhs[:n] + rhs[n:] - apply(start)
        x_s[...] = start
        r_s[...] = resid
        p_s[...] = resid

        def step(_, now):
            direction = p_s[...]
            image = apply(direction)
            alpha = now / jnp.sum(direction * image, axis=1, keepdims=True)
            x_s[...] += alpha * direction
            left = r_s[...] - alpha * image
            r_s[...] = left
            later = jnp.sum(left * left, axis=1, keepdims=True)
            p_s[...] = left + later / now * direction
            return later

        lax.fori_loop(0, CG_STEPS, step, jnp.sum(resid * resid, axis=1, keepdims=True))
        out = x_s[...]
        out_ref[...] = out
        if pack:
            small = out.astype(jnp.bfloat16)
            many = units_of(n)
            for j in range(n // 8):
                piece = small[j // 2 * 16 : j // 2 * 16 + 16, j % 2 * 128 : j % 2 * 128 + 128]
                if j < many[0]:
                    packed[0][j] = piece
                elif j < many[0] + many[1]:
                    packed[1][j - many[0]] = piece
                else:
                    packed[2][j - many[0] - many[1]] = piece


def solve(tables, codes, weights, gains, start, owner_rows, pack):
    n = start.shape[0]
    units = [t.shape[4] for t in tables]
    slots = codes.shape[1]
    depth = 2 * 16 * owner_rows
    whole = lambda shape: pl.BlockSpec(shape, lambda g: (0,) * len(shape))
    table_specs = [
        pl.BlockSpec((1, 4, 4, 2, units[0], 16, 128), lambda g: (g % 2, 0, 0, g // 2, 0, 0, 0)),
        pl.BlockSpec((1, 4, 4, 2, units[1], 16, 128), lambda g: (g % 2, 0, 0, g // 2, 0, 0, 0)),
        pl.BlockSpec((1, 2, 4, 4, units[2], 16, 128), lambda g: (g % 2, g // 2, 0, 0, 0, 0, 0)),
    ]
    out_shape = [jax.ShapeDtypeStruct((n, RANK), jnp.float32)]
    if pack:
        out_shape += [jax.ShapeDtypeStruct((u, 16, 128), jnp.bfloat16) for u in units_of(n)]
    return pl.pallas_call(
        functools.partial(solve_kernel, n, owner_rows, units, pack),
        grid=(8,),
        out_shape=out_shape,
        in_specs=table_specs + [whole(codes.shape)] * 3 + [whole(start.shape)],
        out_specs=[whole(s.shape) for s in out_shape],
        scratch_shapes=[
            pltpu.VMEM((depth, RANK + slots), jnp.bfloat16),
            pltpu.VMEM((RANK, depth), jnp.bfloat16),
            pltpu.VMEM((RANK, 8 * slots), jnp.bfloat16),
            pltpu.VMEM((8 * slots, RANK), jnp.bfloat16),
            pltpu.VMEM((RANK, RANK), jnp.float32),
            pltpu.VMEM((RANK, 2 * RANK), jnp.bfloat16),
            pltpu.VMEM((n, 8 * slots), jnp.float32),
            pltpu.VMEM((n, RANK), jnp.float32),
            pltpu.VMEM((n, RANK), jnp.float32),
            pltpu.VMEM((n, RANK), jnp.float32),
        ],
        compiler_params=pltpu.CompilerParams(
            dimension_semantics=("arbitrary",), vmem_limit_bytes=48 << 20
        ),
        name=f"solve_{n}",
    )(*tables, codes, weights, gains, start)


def slot_rows(array):
    n, blocks, slots = array.shape
    return array.transpose(1, 2, 0).reshape(blocks, slots * n)


def slot_inputs(slot_ids, confidence, slot_mask, owner_rows):
    ids = slot_rows(slot_ids)
    owner, row = ids // owner_rows, ids % owner_rows
    chunk = owner // 16 * (owner_rows // 16) + row // 16
    codes = chunk * 256 + owner % 16 * 16 + row % 16
    mask = slot_rows(slot_mask).astype(jnp.float32)
    conf = slot_rows(confidence)
    return codes, mask * conf, mask * (1.0 + conf)


def per_device(
    user_factors, item_factors, user_items, user_conf, user_mask, item_users, item_conf, item_mask
):
    users, items = user_factors.shape[0], item_factors.shape[0]
    small = item_factors.astype(jnp.bfloat16).reshape(items // 16, 16, 2, 128)
    small = small.transpose(0, 2, 1, 3).reshape(items // 8, 16, 128)
    counts = units_of(items)
    pieces = jnp.split(small, [counts[0], counts[0] + counts[1]])
    tables = gather_table(pieces, 0)
    solved = solve(tables, *slot_inputs(user_items, user_conf, user_mask, items), user_factors, items, True)
    new_users, pieces = solved[0], solved[1:]
    tables = gather_table(pieces, 1)
    new_items = solve(
        tables, *slot_inputs(item_users, item_conf, item_mask, users), item_factors, users, False
    )[0]
    return new_users, new_items


def solution(mesh):
    both = ("grp", "dev")
    two, three = P(both, None), P(both, None, None)
    return jax.shard_map(
        per_device,
        mesh=mesh,
        in_specs=(two, two) + (three,) * 6,
        out_specs=(two, two),
        check_vma=False,
    )
```

```python
import functools

import jax
import jax.numpy as jnp
from jax import lax
from jax.experimental import pallas as pl
from jax.experimental.pallas import tpu as pltpu
from jax.sharding import PartitionSpec as P

MESH = pl.DeviceIdType.MESH
CG_STEPS = 4
RANK = 256
NX, NY, NZ = 4, 4, 8
BLOCKS = 8
SIZES = {"x": NX, "y": NY, "z": NZ}
ORDERS = (("z", "y", "x"), ("z", "x", "y"), ("x", "y", "z"))
SCHEDULE = (
    (2, 0), (0, 0), (1, 0), (2, 1), (0, 1), (1, 1), (2, 0, 0), (2, 0, 1), "own", (2, 1, 0), (2, 1, 1), "z1",
    (0, 0, 0), (1, 0, 0), (2, 2, 0), (2, 2, 1), "z2", (0, 0, 1), (1, 0, 1), "beside", (2, 3, 0), "z3",
    (0, 1, 0), (1, 1, 0), "z4", "across",
)


def units_of(rows):
    units = rows // 16 * 2
    last = units // 4
    side = (units - last) // 2
    return (side, side, last)


def buffer_shape(order, units):
    return (2,) + tuple(SIZES[a] for a in order[::-1]) + (units, 16, 128)


def my_coords():
    grp, dev = lax.axis_index("grp"), lax.axis_index("dev")
    core = grp % 2
    z = grp // 2 * 2 + dev // 16
    return {"core": core, "z": z, "y": dev // 4 % 4, "x": dev % 4}


def device_at(coords):
    return {
        "grp": coords["z"] // 2 * 2 + coords["core"],
        "dev": coords["z"] % 2 * 16 + coords["y"] * 4 + coords["x"],
    }


def moved(me, axis, shift):
    size = SIZES[axis]
    return {**me, axis: (me[axis] + shift + size) % size}


def shifts_of(size):
    far = [size // 2]
    return far + [s for d in range(size // 2 - 1, 0, -1) for s in (d, -d)]


class Gather:
    def __init__(self, pieces, tables, send_sem, recv_sem, local_sem):
        self.pieces, self.tables = pieces, tables
        self.send_sem, self.recv_sem, self.local_sem = send_sem, recv_sem, local_sem
        self.me = my_coords()
        self.partner = device_at({**self.me, "core": 1 - self.me["core"]})
        self.issued, self.flying, self.handed, self.local = [], {}, {}, []

    def greet(self):
        barrier = pltpu.get_barrier_semaphore()
        others = [self.partner]
        for axis, size in SIZES.items():
            others += [device_at(moved(self.me, axis, s)) for s in shifts_of(size)]
        for other in others:
            pl.semaphore_signal(barrier, inc=1, device_id=other, device_id_type=MESH)
        pl.semaphore_wait(barrier, len(others))

    def remote(self, src, dst, target):
        e = len(self.issued)
        copy = pltpu.make_async_remote_copy(
            src_ref=src,
            dst_ref=dst,
            send_sem=self.send_sem.at[e],
            recv_sem=self.recv_sem.at[e],
            device_id=target,
            device_id_type=MESH,
        )
        copy.start()
        self.issued.append(copy)
        return copy

    def block(self, colour, phase, v, half=None):
        order, ref = ORDERS[colour], self.tables[colour]
        index = [self.me["core"]] + [self.me[order[k]] for k in range(2, phase, -1)] + [v]
        if half is not None:
            cut = ref.shape[len(index)] // 2
            index.append(pl.ds(half * cut, cut))
        return ref.at[tuple(index)]

    def send_direct(self, colour, phase):
        axis = ORDERS[colour][phase]
        dst = self.block(colour, phase, self.me[axis])
        src = self.pieces[colour] if phase == 0 else dst
        self.flying[colour, phase] = [
            self.remote(src, dst, device_at(moved(self.me, axis, s)))
            for s in shifts_of(SIZES[axis])
        ]

    def send_ring(self, colour, k, i):
        axis = ORDERS[colour][2]
        if k == SIZES[axis] // 2 - 1 and i == 1 or k == SIZES[axis] // 2:
            return
        pair = []
        for way, shift in enumerate((1, -1)):
            part = self.block(colour, 2, moved(self.me, axis, -shift * k)[axis], way ^ i)
            pair.append(self.remote(part, part, device_at(moved(self.me, axis, shift))))
        self.flying[colour, k, i] = pair

    def begin(self):
        self.greet()
        for colour in (2, 0, 1):
            self.send_direct(colour, 0)
        for colour in range(3):
            own = self.tables[colour].at[
                (self.me["core"],) + tuple(self.me[a] for a in ORDERS[colour][::-1])
            ]
            copy = pltpu.make_async_copy(self.pieces[colour], own, self.local_sem.at[colour])
            copy.start()
            self.local.append(copy)

    def take(self, token):
        colour = token[0]
        for copy in self.flying[token]:
            copy.wait_recv()
        if len(token) == 2:
            phase = token[1]
            if phase == 0:
                self.local[colour].wait()
                self.send_direct(colour, 1)
            else:
                self.send_ring(colour, 0, 0)
                self.send_ring(colour, 0, 1)
                slab = self.block(colour, 2, self.me[ORDERS[colour][2]])
                self.handed[token] = [self.remote(slab, slab, self.partner)]
            return
        k, i = token[1:]
        self.send_ring(colour, k + 1, i)
        axis = ORDERS[colour][2]
        self.handed[token] = []
        for way, shift in enumerate((1, -1)):
            got = self.block(colour, 2, moved(self.me, axis, -shift * (k + 1))[axis], way ^ i)
            self.handed[token].append(self.remote(got, got, self.partner))

    def have(self, token):
        for copy in self.handed.pop(token, ()):
            copy.wait_recv()

    def finish(self):
        for copy in self.issued:
            copy.wait_send()


def gather_copies():
    total = 0
    for order in ORDERS:
        total += SIZES[order[0]] + SIZES[order[1]] - 1
        total += 4 * (SIZES[order[2]] - 1)
    return total


def split_two(value):
    high = value.astype(jnp.bfloat16)
    low = (value - high.astype(jnp.float32)).astype(jnp.bfloat16)
    return jnp.concatenate([high, low], axis=0)


def dot(a, b):
    return jnp.dot(a, b, preferred_element_type=jnp.float32)


def groups_of(rows):
    units = units_of(rows)
    return [u // 2 for u in units], units[0] % 2


def codes_of(ids, rows):
    counts, mixed = groups_of(rows)
    owner, row = ids // rows, ids % rows
    zl, y, x = owner // 16, owner // 4 % 4, owner % 4
    group, r = row // 16, row % 16
    first = x * (128 * counts[0]) + ((zl * 4 + y) * counts[0] + group) * 16 + r
    at = 512 * counts[0]
    base = counts[0] + mixed
    second = at + y * (128 * counts[1]) + ((zl * 4 + x) * counts[1] + group - base) * 16 + r
    at += 512 * counts[1]
    base += counts[1]
    third = at + (((zl * 4 + y) * 4 + x) * counts[2] + group - base) * 16 + r
    at += 512 * counts[2]
    code = jnp.where(group < base, second, third)
    if mixed:
        shared = at + ((zl * 4 + y) * 4 + x) * 16 + r
        code = jnp.where(group == counts[0], shared, code)
    return jnp.where(group < counts[0], first, code)


def half_step_kernel(n, rows, pack, *refs):
    pieces = refs[:3]
    code_ref, weight_ref, gain_ref, start_ref = refs[3:7]
    out_ref = refs[7]
    packed = refs[8:11] if pack else ()
    scratch = refs[8 + len(packed):]
    tables = scratch[:3]
    (acc, gram, gram2, picked_t, picked, diag, gains, x_s, r_s, p_s) = scratch[3:13]
    gather = Gather(pieces, tables, *scratch[13:])
    gather.begin()

    counts, mixed = groups_of(rows)
    slots = code_ref.shape[1]
    total = slots * BLOCKS

    acc[...] = jnp.zeros_like(acc)
    gram[...] = jnp.zeros_like(gram)
    lane = lax.broadcasted_iota(jnp.int32, (n, slots), 1)
    own = lane % n == lax.broadcasted_iota(jnp.int32, (n, slots), 0)
    for g in range(BLOCKS):
        span = slice(g * slots, (g + 1) * slots)
        diag[:, span] = jnp.where(own, weight_ref[g : g + 1, :], 0.0)
        gains[:, span] = split_two(jnp.where(own, gain_ref[g : g + 1, :], 0.0))

    def add(g, parts):
        code = code_ref[pl.ds(g, 1), :]
        chosen, held = [], [[], []]
        for tiles, position in parts:
            where = lax.broadcasted_iota(jnp.int32, (16 * len(tiles), slots), 0) + position
            chosen.append(jnp.where(where == code, 1.0, 0.0).astype(jnp.bfloat16))
            for h in (0, 1):
                held[h] += [t[h] for t in tiles]
        part = jnp.concatenate([jnp.concatenate(t, axis=0) for t in held], axis=1)
        hot = jnp.concatenate(chosen, axis=0)
        product = dot(part.T, jnp.concatenate([part, hot], axis=1))
        gram[...] += product[:, 0:RANK]
        lanes = pl.ds(pl.multiple_of(g * slots, 128), slots)
        acc[:, lanes] += product[:, RANK : RANK + slots]

    me = gather.me

    def side_part(g, colour, shift):
        v = moved(me, ORDERS[colour][2], shift)[ORDERS[colour][2]]
        table, count = tables[colour], counts[colour]
        skip = mixed if colour == 1 else 0
        core, z = g % 2, g // 2 * 2
        tiles = [
            [table[core, v, a, z + zl, skip + 2 * q + h] for h in (0, 1)]
            for zl in (0, 1) for a in range(4) for q in range(count)
        ]
        return tiles, 512 * sum(counts[:colour]) + v * (128 * count)

    def shared_part(g):
        core, z = g % 2, g // 2 * 2
        tiles = [
            [tables[0][core, x, y, z + zl, 2 * counts[0]], tables[1][core, y, x, z + zl, 0]]
            for zl in (0, 1) for y in range(NY) for x in range(NX)
        ]
        return tiles, 512 * sum(counts)

    def sides(shifts, last=False):
        def block(g, _):
            parts = [side_part(g, colour, s) for colour in (0, 1) for s in shifts]
            add(g, parts + ([shared_part(g)] if last and mixed else []))
            return 0

        lax.fori_loop(0, BLOCKS, block, 0)

    def level(shift):
        v, table, count = moved(me, "z", shift)["z"], tables[2], counts[2]

        def one(core, _):
            tiles = [
                [table[core, v, y, x, 2 * q + h] for h in (0, 1)]
                for y in range(NY) for x in range(NX) for q in range(count)
            ]
            add(v // 2 * 2 + core, [(tiles, 512 * sum(counts[:2]) + v % 2 * (256 * count))])
            return 0

        lax.fori_loop(0, 2, one, 0)

    work = {
        "own": ([(0, 1), (1, 1), (2, 1)], lambda: (sides((0,)), level(0))),
        "z1": ([(2, 0, 0), (2, 0, 1)], lambda: (level(1), level(-1))),
        "z2": ([(2, 1, 0), (2, 1, 1)], lambda: (level(2), level(-2))),
        "z3": ([(2, 2, 0), (2, 2, 1)], lambda: (level(3), level(-3))),
        "z4": ([(2, 3, 0)], lambda: level(4)),
        "beside": ([(0, 0, 0), (0, 0, 1), (1, 0, 0), (1, 0, 1)], lambda: sides((1, -1))),
        "across": ([(0, 1, 0), (1, 1, 0)], lambda: sides((2,), last=True)),
    }
    for token in SCHEDULE:
        if token in work:
            needs, run = work[token]
            for need in needs:
                gather.have(need)
            run()
        else:
            gather.take(token)

    for g in range(BLOCKS):
        span = slice(g * slots, (g + 1) * slots)
        here = acc[:, span]
        picked_t[:, span] = here.astype(jnp.bfloat16)
        picked[span, :] = here.T.astype(jnp.bfloat16)
    whole = gram[...]
    high = whole.astype(jnp.bfloat16)
    gram2[:, 0:RANK] = high
    gram2[:, RANK : 2 * RANK] = (whole - high.astype(jnp.float32)).astype(jnp.bfloat16)
    width = 768

    def apply(vector):
        two = split_two(vector)
        by_gram = dot(two, gram2[...])
        image = by_gram[:n, :RANK] + by_gram[:n, RANK:] + by_gram[n:, :RANK] + vector
        extra = jnp.zeros((2 * n, RANK), jnp.float32)
        for at in range(0, total, width):
            along = dot(two, picked_t[:, at : at + width])
            along = (along[:n] + along[n:]) * diag[:, at : at + width]
            extra = extra + dot(split_two(along), picked[at : at + width, :])
        return image + extra[:n] + extra[n:]

    rhs = dot(gains[...], picked[...])
    start = start_ref[...]
    resid = rhs[:n] + rhs[n:] - apply(start)
    x_s[...] = start
    r_s[...] = resid
    p_s[...] = resid

    def step(_, now):
        direction = p_s[...]
        image = apply(direction)
        alpha = now / jnp.sum(direction * image, axis=1, keepdims=True)
        x_s[...] += alpha * direction
        left = r_s[...] - alpha * image
        r_s[...] = left
        later = jnp.sum(left * left, axis=1, keepdims=True)
        p_s[...] = left + later / now * direction
        return later

    lax.fori_loop(0, CG_STEPS, step, jnp.sum(resid * resid, axis=1, keepdims=True))
    out = x_s[...]
    out_ref[...] = out
    if pack:
        small = out.astype(jnp.bfloat16)
        many = units_of(n)
        for j in range(n // 8):
            piece = small[j // 2 * 16 : j // 2 * 16 + 16, j % 2 * 128 : j % 2 * 128 + 128]
            if j < many[0]:
                packed[0][j] = piece
            elif j < many[0] + many[1]:
                packed[1][j - many[0]] = piece
            else:
                packed[2][j - many[0] - many[1]] = piece
    gather.finish()


def half_step(pieces, codes, weights, gains, start, rows, pack):
    n, slots = start.shape[0], codes.shape[1]
    units = units_of(rows)
    total = BLOCKS * slots
    out_shape = [jax.ShapeDtypeStruct((n, RANK), jnp.float32)]
    if pack:
        out_shape += [jax.ShapeDtypeStruct((u, 16, 128), jnp.bfloat16) for u in units_of(n)]
    near = pl.BlockSpec(memory_space=pltpu.VMEM)
    copies = gather_copies()
    return pl.pallas_call(
        functools.partial(half_step_kernel, n, rows, pack),
        out_shape=out_shape,
        in_specs=[pl.BlockSpec(memory_space=pl.ANY)] * 3 + [near] * 4,
        out_specs=[near] * len(out_shape),
        scratch_shapes=[
            *(pltpu.VMEM(buffer_shape(o, u), jnp.bfloat16) for o, u in zip(ORDERS, units)),
            pltpu.VMEM((RANK, total), jnp.float32),
            pltpu.VMEM((RANK, RANK), jnp.float32),
            pltpu.VMEM((RANK, 2 * RANK), jnp.bfloat16),
            pltpu.VMEM((RANK, total), jnp.bfloat16),
            pltpu.VMEM((total, RANK), jnp.bfloat16),
            pltpu.VMEM((n, total), jnp.float32),
            pltpu.VMEM((2 * n, total), jnp.bfloat16),
            pltpu.VMEM((n, RANK), jnp.float32),
            pltpu.VMEM((n, RANK), jnp.float32),
            pltpu.VMEM((n, RANK), jnp.float32),
            pltpu.SemaphoreType.DMA((copies,)),
            pltpu.SemaphoreType.DMA((copies,)),
            pltpu.SemaphoreType.DMA((3,)),
        ],
        compiler_params=pltpu.CompilerParams(
            collective_id=0 if pack else 1, has_side_effects=True, vmem_limit_bytes=56 << 20
        ),
        name=f"half_step_{n}",
    )(*pieces, codes, weights, gains, start)


def slot_rows(array):
    n, blocks, slots = array.shape
    return array.transpose(1, 2, 0).reshape(blocks, slots * n)


def slot_inputs(slot_ids, confidence, slot_mask, rows):
    mask = slot_rows(slot_mask).astype(jnp.float32)
    conf = slot_rows(confidence)
    return codes_of(slot_rows(slot_ids), rows), mask * conf, mask * (1.0 + conf)


def per_device(
    user_factors, item_factors, user_items, user_conf, user_mask, item_users, item_conf, item_mask
):
    users, items = user_factors.shape[0], item_factors.shape[0]
    small = item_factors.astype(jnp.bfloat16).reshape(items // 16, 16, 2, 128)
    small = small.transpose(0, 2, 1, 3).reshape(items // 8, 16, 128)
    counts = units_of(items)
    pieces = jnp.split(small, [counts[0], counts[0] + counts[1]])
    inputs = slot_inputs(user_items, user_conf, user_mask, items)
    solved = half_step(pieces, *inputs, user_factors, items, True)
    inputs = slot_inputs(item_users, item_conf, item_mask, users)
    new_items = half_step(solved[1:], *inputs, item_factors, users, False)[0]
    return solved[0], new_items


def solution(mesh):
    both = ("grp", "dev")
    two, three = P(both, None), P(both, None, None)
    return jax.shard_map(
        per_device,
        mesh=mesh,
        in_specs=(two, two) + (three,) * 6,
        out_specs=(two, two),
        check_vma=False,
    )
```

```python
import functools

import jax
import jax.numpy as jnp
from jax import lax
from jax.experimental import pallas as pl
from jax.experimental.pallas import tpu as pltpu
from jax.sharding import PartitionSpec as P

MESH = pl.DeviceIdType.MESH
CG_STEPS = 4
RANK = 256
NX, NY, NZ = 4, 4, 8
BLOCKS = 8
SIZES = {"x": NX, "y": NY, "z": NZ}
ORDERS = (("z", "y", "x"), ("z", "x", "y"), ("x", "y", "z"))
SCHEDULES = {
    64: (
        ("f", 2), ("f", 0), ("s", 2, -1), ("s", 2, 1), (2, 0, 0), ("f", 1), ("s", 2, 2), ("s", 0, -1), ("s", 0, 1), (0,
        0, 0), (2, 0, -1), ("w", "z", 0), (2, 0, 1), (2, 1, 0), ("s", 1, -1), ("s", 1, 1), (2, 0, 2), ("w", "z", 1), (2,
        1, -1), ("s", 0, 2), (2, 1, 1), ("w", "z", -1), (2, 2, 0), (1, 0, 0), (2, 1, 2), ("s", 1, 2), (1, 0, -1), (0, 0,
        -1), ("w", "z", 2), (2, 2, -1), (2, 2, 1), ("w", "own", 0), (1, 0, 1), (2, 3, 0), (0, 0, 1), ("w", "own", 1),
        (2, 2, 2), ("w", "own", 2), (1, 1, 0), (0, 1, 0), (2, 3, -1), ("w", "own", 3), (2, 3, 1), (1, 0, 2), (0, 1, -1),
        (0, 0, 2), ("w", "z", -2), (1, 1, -1), (2, 3, 2), ("w", "z", 3), (0, 1, 1), ("w", "z", -3), (1, 1, 1), ("w",
        "beside", 0), ("w", "beside", 1), (1, 1, 2), (0, 1, 2), ("w", "beside", 2), ("w", "beside", 3), ("w", "z", 4)
    ),
    128: (
        ("f", 2), ("f", 0), ("s", 2, -1), ("s", 2, 1), ("f", 1), (2, 0, 0), (2, 0, -1), ("s", 0, -1), ("s", 0, 1), (0,
        0, 0), ("s", 2, 2), (2, 0, 1), ("w", "z", 0), (2, 1, 0), (2, 1, -1), ("s", 1, -1), ("s", 1, 1), (1, 0, 0), (2,
        0, 2), ("s", 0, 2), (2, 1, 1), ("w", "z", 1), (2, 2, 0), (0, 0, -1), ("w", "z", -1), (2, 2, -1), (2, 1, 2), (1,
        0, -1), (2, 2, 1), (0, 0, 1), ("w", "z", 2), (2, 3, 0), (2, 3, -1), ("w", "z", -2), (2, 2, 2), (1, 0, 1), (0, 1,
        0), (2, 3, 1), ("w", "z", 3), ("s", 1, 2), ("w", "z", -3), (1, 1, 0), (1, 1, -1), (2, 3, 2), ("w", "own", 0),
        (0, 0, 2), (0, 1, -1), ("w", "own", 1), (1, 1, 1), ("w", "own", 2), ("w", "z", 4), (0, 1, 1), (1, 0, 2), ("w",
        "own", 3), (0, 1, 2), ("w", "beside", 0), ("w", "beside", 1), (1, 1, 2), ("w", "beside", 2), ("w", "beside", 3)
    ),
}


def units_of(rows):
    units = rows // 16 * 2
    last = units // 4
    side = (units - last) // 2
    return (side, side, last)


def buffer_shape(order, units):
    return (2,) + tuple(SIZES[a] for a in order[::-1]) + (units, 16, 128)


def my_coords():
    grp, dev = lax.axis_index("grp"), lax.axis_index("dev")
    core = grp % 2
    z = grp // 2 * 2 + dev // 16
    return {"core": core, "z": z, "y": dev // 4 % 4, "x": dev % 4}


def device_at(coords):
    return {
        "grp": coords["z"] // 2 * 2 + coords["core"],
        "dev": coords["z"] % 2 * 16 + coords["y"] * 4 + coords["x"],
    }


def moved(me, axis, shift):
    size = SIZES[axis]
    return {**me, axis: (me[axis] + shift + size) % size}


def shifts_of(size):
    far = [size // 2]
    return far + [s for d in range(size // 2 - 1, 0, -1) for s in (d, -d)]


class Gather:
    def __init__(self, ring, pieces, tables, send_sem, recv_sem, local_sem):
        self.ring = ring
        self.pieces, self.tables = pieces, tables
        self.send_sem, self.recv_sem, self.local_sem = send_sem, recv_sem, local_sem
        self.me = my_coords()
        self.partner = device_at({**self.me, "core": 1 - self.me["core"]})
        self.issued, self.flying, self.handed, self.local = [], {}, {}, {}

    def greet(self):
        barrier = pltpu.get_barrier_semaphore()
        others = [self.partner]
        for axis, size in SIZES.items():
            others += [device_at(moved(self.me, axis, s)) for s in shifts_of(size)]
        for other in others:
            pl.semaphore_signal(barrier, inc=1, device_id=other, device_id_type=MESH)
        pl.semaphore_wait(barrier, len(others))

    def remote(self, src, dst, target):
        e = len(self.issued)
        copy = pltpu.make_async_remote_copy(
            src_ref=src,
            dst_ref=dst,
            send_sem=self.send_sem.at[e],
            recv_sem=self.recv_sem.at[e],
            device_id=target,
            device_id_type=MESH,
        )
        copy.start()
        self.issued.append(copy)
        return copy

    def send_first(self, colour):
        axis = ORDERS[colour][0]
        dst = self.tables[colour].at[
            (self.me["core"],) + tuple(self.me[a] for a in ORDERS[colour][::-1])
        ]
        self.flying["f", colour] = [
            self.remote(self.pieces[colour], dst, device_at(moved(self.me, axis, s)))
            for s in shifts_of(SIZES[axis])
        ]
        return dst

    def quarter(self, colour, far, s, half=None):
        _, second, last = ORDERS[colour]
        index = (self.me["core"], moved(self.me, last, far)[last], moved(self.me, second, s)[second])
        if half is not None:
            cut = self.tables[colour].shape[3] // 2
            index += (pl.ds(half * cut, cut),)
        return self.tables[colour].at[index]

    def send_second(self, colour):
        axis = ORDERS[colour][1]
        part = self.quarter(colour, 0, 0)
        for s in (1, -1) if self.ring else (1, -1, 2):
            copy = self.remote(part, part, device_at(moved(self.me, axis, s)))
            self.flying["s", colour, 2 if s == 2 else -s] = [copy]

    def send_last(self, colour, k, s):
        axis = ORDERS[colour][2]
        steps = SIZES[axis] // 2
        if k == steps:
            return
        sent = []
        for way, shift in enumerate((1, -1)):
            if k < steps - 1 or way == s % 2:
                part = self.quarter(colour, -shift * k, s)
                got = self.quarter(colour, -shift * (k + 1), s)
                sent.append((self.remote(part, part, device_at(moved(self.me, axis, shift))), got))
        self.flying[colour, k, s] = sent

    def begin(self):
        self.greet()
        for colour in (2, 0, 1):
            own = self.send_first(colour)
            copy = pltpu.make_async_copy(self.pieces[colour], own, self.local_sem.at[colour])
            copy.start()
            self.local[colour] = copy

    def take(self, token):
        if token[0] == "f":
            colour = token[1]
            for copy in self.flying[token]:
                copy.wait_recv()
            self.local[colour].wait()
            self.send_second(colour)
            self.send_last(colour, 0, 0)
        elif token[0] == "s":
            colour, s = token[1:]
            for copy in self.flying[token]:
                copy.wait_recv()
            if self.ring and s != 2:
                axis = ORDERS[colour][1]
                half = 0 if s == -1 else 1
                part = self.quarter(colour, 0, s, half)
                copy = self.remote(part, part, device_at(moved(self.me, axis, -s)))
                self.flying.setdefault(("s", colour, 2), []).append(copy)
            self.send_last(colour, 0, s)
            if s == 2:
                slab = self.tables[colour].at[self.me["core"], self.me[ORDERS[colour][2]]]
                self.handed[token] = [self.remote(slab, slab, self.partner)]
        else:
            colour, k, s = token
            arrived = self.flying[token]
            for copy, _ in arrived:
                copy.wait_recv()
            self.send_last(colour, k + 1, s)
            self.handed[token] = [self.remote(got, got, self.partner) for _, got in arrived]

    def have(self, token):
        for copy in self.handed.pop(token, ()):
            copy.wait_recv()

    def finish(self):
        for copy in self.issued:
            copy.wait_send()


def gather_copies():
    return 1 + sum(SIZES[o[0]] + SIZES[o[1]] + 1 + 12 * (SIZES[o[2]] - 2) for o in ORDERS)


def split_two(value):
    high = value.astype(jnp.bfloat16)
    low = (value - high.astype(jnp.float32)).astype(jnp.bfloat16)
    return jnp.concatenate([high, low], axis=0)


def dot(a, b):
    return jnp.dot(a, b, preferred_element_type=jnp.float32)


def groups_of(rows):
    units = units_of(rows)
    return [u // 2 for u in units], units[0] % 2


def codes_of(ids, rows):
    counts, mixed = groups_of(rows)
    bits = rows.bit_length() - 1
    owner, row = ids >> bits, ids & (rows - 1)
    zl, y, x = owner >> 4, (owner >> 2) & 3, owner & 3
    group, r = row >> 4, row & 15
    first = x * (128 * counts[0]) + ((zl * 4 + y) * counts[0] + group) * 16 + r
    at = 512 * counts[0]
    base = counts[0] + mixed
    second = at + y * (128 * counts[1]) + ((zl * 4 + x) * counts[1] + group - base) * 16 + r
    at += 512 * counts[1]
    base += counts[1]
    third = at + (((zl * 4 + y) * 4 + x) * counts[2] + group - base) * 16 + r
    at += 512 * counts[2]
    code = jnp.where(group < base, second, third)
    if mixed:
        shared = at + ((zl * 4 + y) * 4 + x) * 16 + r
        code = jnp.where(group == counts[0], shared, code)
    return jnp.where(group < counts[0], first, code)


def half_step_kernel(n, rows, pack, *refs):
    pieces_ref, ids_ref, conf_ref, mask_ref, start_ref, out_ref = refs[:6]
    packed = refs[6] if pack else None
    scratch = refs[7:] if pack else refs[6:]
    pieces, at = [], 0
    for u in units_of(rows):
        pieces.append(pieces_ref.at[pl.ds(at, u)])
        at += u
    tables = scratch[:3]
    (acc, gram, other, gram2, picked_t, picked, diag, gains, columns, x_s, r_s, p_s) = scratch[3:15]
    gather = Gather(not pack, pieces, tables, *scratch[15:])
    gather.begin()

    counts, mixed = groups_of(rows)
    slots = n * ids_ref.shape[0]

    def along_lanes(ref):
        return jnp.concatenate([ref[k] for k in range(ref.shape[0])], axis=1)

    code = codes_of(along_lanes(ids_ref), rows)
    mask = along_lanes(mask_ref).astype(jnp.float32)
    conf = along_lanes(conf_ref)
    weight, gain = mask * conf, mask * (1.0 + conf)
    total = slots * BLOCKS

    acc[...] = jnp.zeros_like(acc)
    gram[...] = jnp.zeros_like(gram)
    lane = lax.broadcasted_iota(jnp.int32, (n, slots), 1)
    own = lane % n == lax.broadcasted_iota(jnp.int32, (n, slots), 0)
    for g in range(BLOCKS):
        span = slice(g * slots, (g + 1) * slots)
        diag[:, span] = jnp.where(own, weight[g : g + 1, :], 0.0)
        gains[:, span] = split_two(jnp.where(own, gain[g : g + 1, :], 0.0))
        for at in range(0, slots, 128):
            row = jnp.broadcast_to(code[g : g + 1, at : at + 128], (128, 128))
            columns[pl.ds(g * slots + at, 128), :] = row.T

    def add(g, parts, with_gram):
        at = pl.ds(pl.multiple_of(g * slots, 128), slots)
        code = columns[at, :]
        lane = lax.broadcasted_iota(jnp.int32, (slots, 128), 1)
        chosen, held = [], [[], []]
        for tiles, position in parts:
            for first in range(0, 16 * len(tiles), 128):
                hit = lane + (position + first) == code
                chosen.append(jnp.where(hit, 1.0, 0.0).astype(jnp.bfloat16))
            for h in (0, 1):
                held[h] += [t[h] for t in tiles]
        part = jnp.concatenate([jnp.concatenate(t, axis=0) for t in held], axis=1)
        if with_gram:
            gram[...] += dot(part.T, part)
        acc[at, :] += dot(jnp.concatenate(chosen, axis=1), part)

    me = gather.me

    def side_part(g, colour, shift):
        v = moved(me, ORDERS[colour][2], shift)[ORDERS[colour][2]]
        table, count = tables[colour], counts[colour]
        skip = mixed if colour == 1 else 0
        core, z = g % 2, g // 2 * 2
        tiles = [
            [table[core, v, a, z + zl, skip + 2 * q + h] for h in (0, 1)]
            for zl in (0, 1) for a in range(4) for q in range(count)
        ]
        return tiles, 512 * sum(counts[:colour]) + v * (128 * count)

    def shared_part(g):
        core, z = g % 2, g // 2 * 2
        tiles = [
            [tables[0][core, x, y, z + zl, 2 * counts[0]], tables[1][core, y, x, z + zl, 0]]
            for zl in (0, 1) for y in range(NY) for x in range(NX)
        ]
        return tiles, 512 * sum(counts)

    def sides(shifts, pair, last=False):
        for mine in (True, False):
            g = 2 * pair + (me["core"] if mine else 1 - me["core"])
            parts = [side_part(g, colour, s) for colour in (0, 1) for s in shifts]
            add(g, parts + ([shared_part(g)] if last and mixed else []), mine)

    def level(shift):
        v, table, count = moved(me, "z", shift)["z"], tables[2], counts[2]
        for mine in (True, False):
            core = me["core"] if mine else 1 - me["core"]
            tiles = [
                [table[core, v, y, x, 2 * q + h] for h in (0, 1)]
                for y in range(NY) for x in range(NX) for q in range(count)
            ]
            position = 512 * sum(counts[:2]) + v % 2 * (256 * count)
            add(v // 2 * 2 + core, [(tiles, position)], mine)

    def across(pair, _):
        sides((2,), pair, last=True)
        return 0

    def work(what, which):
        every = (0, 1, -1, 2)
        if what == "own":
            needs, run = [("s", c, 2) for c in (0, 1)], lambda: sides((0,), which)
        elif what == "beside":
            needs = [(c, 0, s) for c in (0, 1) for s in every]
            run = lambda: sides((1, -1), which)
        elif what == "across":
            needs, run = [(c, 1, s) for c in (0, 1) for s in every], lambda: lax.fori_loop(0, BLOCKS // 2, across, 0)
        else:
            needs = [(2, abs(which) - 1, s) for s in every] if which else [("s", 2, 2)]
            run = lambda: level(which)
        for need in needs:
            gather.have(need)
        run()

    for token in SCHEDULES[rows] + (("w", "across", 0),):
        if token[0] == "w":
            work(*token[1:])
        else:
            gather.take(token)

    for g in range(BLOCKS):
        span = slice(g * slots, (g + 1) * slots)
        here = acc[span, :]
        picked[span, :] = here.astype(jnp.bfloat16)
        picked_t[:, span] = here.T.astype(jnp.bfloat16)
        if g == 1:
            swap = gather.remote(gram, other, gather.partner)
    rhs = dot(gains[...], picked[...])
    swap.wait_recv()
    whole = gram[...] + other[...]
    high = whole.astype(jnp.bfloat16)
    gram2[:, 0:RANK] = high
    gram2[:, RANK : 2 * RANK] = (whole - high.astype(jnp.float32)).astype(jnp.bfloat16)
    width = 768

    def apply(vector):
        two = split_two(vector)
        by_gram = dot(two, gram2[...])
        image = by_gram[:n, :RANK] + by_gram[:n, RANK:] + by_gram[n:, :RANK] + vector
        extra = jnp.zeros((2 * n, RANK), jnp.float32)
        for at in range(0, total, width):
            along = dot(two, picked_t[:, at : at + width])
            along = (along[:n] + along[n:]) * diag[:, at : at + width]
            extra = extra + dot(split_two(along), picked[at : at + width, :])
        return image + extra[:n] + extra[n:]

    start = start_ref[...]
    resid = rhs[:n] + rhs[n:] - apply(start)
    x_s[...] = start
    r_s[...] = resid
    p_s[...] = resid

    def step(_, now):
        direction = p_s[...]
        image = apply(direction)
        alpha = now / jnp.sum(direction * image, axis=1, keepdims=True)
        x_s[...] += alpha * direction
        left = r_s[...] - alpha * image
        r_s[...] = left
        later = jnp.sum(left * left, axis=1, keepdims=True)
        p_s[...] = left + later / now * direction
        return later

    lax.fori_loop(0, CG_STEPS, step, jnp.sum(resid * resid, axis=1, keepdims=True))
    out = x_s[...]
    out_ref[...] = out
    if pack:
        small = out.astype(jnp.bfloat16)
        for j in range(n // 8):
            packed[j] = small[j // 2 * 16 : j // 2 * 16 + 16, j % 2 * 128 : j % 2 * 128 + 128]
    gather.finish()


def half_step(pieces, slot_arrays, start, rows, pack):
    n, slots = start.shape[0], start.shape[0] * slot_arrays[0].shape[2]
    units = units_of(rows)
    total = BLOCKS * slots
    out_shape = [jax.ShapeDtypeStruct((n, RANK), jnp.float32)]
    if pack:
        out_shape.append(jax.ShapeDtypeStruct((n // 8, 16, 128), jnp.bfloat16))
    near = pl.BlockSpec(memory_space=pltpu.VMEM)
    copies = gather_copies()
    return pl.pallas_call(
        functools.partial(half_step_kernel, n, rows, pack),
        out_shape=out_shape,
        in_specs=[pl.BlockSpec(memory_space=pl.ANY)] + [near] * 4,
        out_specs=[near] * len(out_shape),
        scratch_shapes=[
            *(pltpu.VMEM(buffer_shape(o, u), jnp.bfloat16) for o, u in zip(ORDERS, units)),
            pltpu.VMEM((total, RANK), jnp.float32),
            pltpu.VMEM((RANK, RANK), jnp.float32),
            pltpu.VMEM((RANK, RANK), jnp.float32),
            pltpu.VMEM((RANK, 2 * RANK), jnp.bfloat16),
            pltpu.VMEM((RANK, total), jnp.bfloat16),
            pltpu.VMEM((total, RANK), jnp.bfloat16),
            pltpu.VMEM((n, total), jnp.float32),
            pltpu.VMEM((2 * n, total), jnp.bfloat16),
            pltpu.VMEM((total, 128), jnp.int32),
            pltpu.VMEM((n, RANK), jnp.float32),
            pltpu.VMEM((n, RANK), jnp.float32),
            pltpu.VMEM((n, RANK), jnp.float32),
            pltpu.SemaphoreType.DMA((copies,)),
            pltpu.SemaphoreType.DMA((copies,)),
            pltpu.SemaphoreType.DMA((3,)),
        ],
        compiler_params=pltpu.CompilerParams(
            collective_id=0 if pack else 1, has_side_effects=True, vmem_limit_bytes=60 << 20
        ),
        name=f"half_step_{n}",
    )(pieces, *(a.transpose(2, 1, 0) for a in slot_arrays), start)


def per_device(
    user_factors, item_factors, user_items, user_conf, user_mask, item_users, item_conf, item_mask
):
    users, items = user_factors.shape[0], item_factors.shape[0]
    small = item_factors.astype(jnp.bfloat16).reshape(items // 16, 16, 2, 128)
    small = small.transpose(0, 2, 1, 3).reshape(items // 8, 16, 128)
    new_users, pieces = half_step(small, (user_items, user_conf, user_mask), user_factors, items, True)
    new_items = half_step(pieces, (item_users, item_conf, item_mask), item_factors, users, False)[0]
    return new_users, new_items


def solution(mesh):
    both = ("grp", "dev")
    two, three = P(both, None), P(both, None, None)
    return jax.shard_map(
        per_device,
        mesh=mesh,
        in_specs=(two, two) + (three,) * 6,
        out_specs=(two, two),
        check_vma=False,
    )
```

```python
import functools

import jax
import jax.numpy as jnp
from jax import lax
from jax.experimental import pallas as pl
from jax.experimental.pallas import tpu as pltpu
from jax.sharding import PartitionSpec as P

MESH = pl.DeviceIdType.MESH
CG_STEPS = 4
RANK = 256
NX, NY, NZ = 4, 4, 8
BLOCKS = 8
SIZES = {"x": NX, "y": NY, "z": NZ}
ORDERS = (("y", "z", "x"), ("z", "x", "y"), ("x", "y", "z"))
SCHEDULES = {
    64: (
        ("f", 2), ("f", 0), ("f", 1), ("s", 2, -1), ("s", 2, 1), (2, 0, 0), (0, 0, 0), ("s", 0, -1), ("s", 0, 1), ("s",
        2, 2), ("w", "z", 0), ("s", 1, -1), ("s", 1, 1), (1, 0, 0), (2, 0, -1), (2, 0, 1), (2, 1, 0), ("s", 0, -2),
        ("s", 0, 2), (2, 0, 2), (2, 1, -1), ("s", 1, 2), (0, 1, 0), ("w", "z", 1), (2, 1, 1), (1, 0, -1), (2, 2, 0), (0,
        0, -1), ("w", "z", -1), (0, 0, 1), ("s", 0, -3), ("s", 0, 3), (1, 0, 1), (2, 1, 2), (0, 0, -2), (2, 2, -1), (0,
        0, 2), ("w", "z", 2), (2, 2, 1), (1, 1, 0), (2, 3, 0), ("w", "z", -2), (0, 1, -1), ("s", 0, 4), (1, 0, 2), (0,
        1, 1), (2, 2, 2), (1, 1, -1), (0, 0, -3), ("w", "own", 0), (2, 3, -1), (0, 0, 3), (2, 3, 1), (0, 1, -2), ("w",
        "own", 1), (1, 1, 1), (0, 1, 2), ("w", "own", 2), ("w", "own", 3), (0, 0, 4), (2, 3, 2), ("w", "z", 3), (1, 1,
        2), (0, 1, -3), ("w", "z", -3), (0, 1, 3), ("w", "beside", 0), ("w", "beside", 1), (0, 1, 4), ("w", "beside",
        2), ("w", "beside", 3), ("w", "z", 4)
    ),
    128: (
        ("f", 2), ("f", 0), ("f", 1), ("s", 2, -1), ("s", 2, 1), (2, 0, 0), (0, 0, 0), ("s", 0, -1), ("s", 0, 1), (2, 0,
        -1), (2, 0, 1), ("s", 1, -1), ("s", 1, 1), (1, 0, 0), ("s", 2, 2), (2, 1, 0), (0, 1, 0), ("w", "z", 0), ("s", 0,
        -2), ("s", 0, 2), (0, 0, -1), (2, 1, -1), (2, 1, 1), (0, 0, 1), (2, 0, 2), (1, 0, -1), ("s", 1, 2), (2, 2, 0),
        ("w", "z", 1), ("w", "z", -1), (0, 0, -2), ("s", 0, -3), ("s", 0, 3), (1, 0, 1), (2, 2, -1), (0, 0, 2), (0, 1,
        -1), (2, 2, 1), (2, 1, 2), (0, 1, 1), (1, 1, 0), (1, 1, -1), (0, 1, -2), (2, 3, 0), ("w", "z", 2), ("s", 0, 4),
        (2, 3, -1), ("w", "z", -2), (0, 0, -3), (2, 3, 1), ("w", "own", 0), (2, 2, 2), (1, 0, 2), (0, 0, 3), ("w",
        "own", 1), (0, 1, 2), ("w", "own", 2), ("w", "z", 3), (1, 1, 1), (0, 0, 4), (2, 3, 2), (0, 1, -3), ("w", "own",
        3), ("w", "z", -3), (0, 1, 3), (1, 1, 2), ("w", "beside", 0), (0, 1, 4), ("w", "beside", 1), ("w", "beside", 2),
        ("w", "beside", 3), ("w", "z", 4)
    ),
}


def units_of(rows):
    units = rows // 16 * 2
    last = units // 4
    side = (units - last) // 2
    return (side, side, last)


def buffer_shape(order, units):
    return (2,) + tuple(SIZES[a] for a in order[::-1]) + (units, 16, 128)


def my_coords():
    grp, dev = lax.axis_index("grp"), lax.axis_index("dev")
    core = grp % 2
    z = grp // 2 * 2 + dev // 16
    return {"core": core, "z": z, "y": dev // 4 % 4, "x": dev % 4}


def device_at(coords):
    return {
        "grp": coords["z"] // 2 * 2 + coords["core"],
        "dev": coords["z"] % 2 * 16 + coords["y"] * 4 + coords["x"],
    }


def moved(me, axis, shift):
    size = SIZES[axis]
    return {**me, axis: (me[axis] + shift + size) % size}


def parts_of(colour):
    size = SIZES[ORDERS[colour][1]]
    return (0,) + tuple(shifts_of(size))


def shifts_of(size):
    far = [size // 2]
    return far + [s for d in range(size // 2 - 1, 0, -1) for s in (d, -d)]


class Gather:
    def __init__(self, ring, pieces, tables, send_sem, recv_sem, local_sem):
        self.ring = ring
        self.pieces, self.tables = pieces, tables
        self.send_sem, self.recv_sem, self.local_sem = send_sem, recv_sem, local_sem
        self.me = my_coords()
        self.partner = device_at({**self.me, "core": 1 - self.me["core"]})
        self.issued, self.flying, self.handed, self.local = [], {}, {}, {}

    def greet(self):
        barrier = pltpu.get_barrier_semaphore()
        others = [self.partner]
        for axis, size in SIZES.items():
            others += [device_at(moved(self.me, axis, s)) for s in shifts_of(size)]
        for other in others:
            pl.semaphore_signal(barrier, inc=1, device_id=other, device_id_type=MESH)
        pl.semaphore_wait(barrier, len(others))

    def remote(self, src, dst, target):
        e = len(self.issued)
        copy = pltpu.make_async_remote_copy(
            src_ref=src,
            dst_ref=dst,
            send_sem=self.send_sem.at[e],
            recv_sem=self.recv_sem.at[e],
            device_id=target,
            device_id_type=MESH,
        )
        copy.start()
        self.issued.append(copy)
        return copy

    def send_first(self, colour):
        axis = ORDERS[colour][0]
        dst = self.tables[colour].at[
            (self.me["core"],) + tuple(self.me[a] for a in ORDERS[colour][::-1])
        ]
        self.flying["f", colour] = [
            self.remote(self.pieces[colour], dst, device_at(moved(self.me, axis, s)))
            for s in shifts_of(SIZES[axis])
        ]
        return dst

    def quarter(self, colour, far, s, half=None):
        _, second, last = ORDERS[colour]
        index = (self.me["core"], moved(self.me, last, far)[last], moved(self.me, second, s)[second])
        if half is not None:
            cut = self.tables[colour].shape[3] // 2
            index += (pl.ds(half * cut, cut),)
        return self.tables[colour].at[index]

    def rings(self, colour):
        return self.ring or SIZES[ORDERS[colour][1]] > 4

    def send_second(self, colour):
        axis = ORDERS[colour][1]
        part = self.quarter(colour, 0, 0)
        for s in (1, -1) if self.rings(colour) else (1, -1, 2):
            copy = self.remote(part, part, device_at(moved(self.me, axis, s)))
            self.flying["s", colour, 2 if s == 2 else -s] = [copy]

    def send_last(self, colour, k, s):
        axis = ORDERS[colour][2]
        steps = SIZES[axis] // 2
        if k == steps:
            return
        sent = []
        for way, shift in enumerate((1, -1)):
            if k < steps - 1 or way == s % 2:
                part = self.quarter(colour, -shift * k, s)
                got = self.quarter(colour, -shift * (k + 1), s)
                sent.append((self.remote(part, part, device_at(moved(self.me, axis, shift))), got))
        self.flying[colour, k, s] = sent

    def begin(self):
        self.greet()
        for colour in (2, 0, 1):
            own = self.send_first(colour)
            copy = pltpu.make_async_copy(self.pieces[colour], own, self.local_sem.at[colour])
            copy.start()
            self.local[colour] = copy

    def take(self, token):
        if token[0] == "f":
            colour = token[1]
            for copy in self.flying[token]:
                copy.wait_recv()
            self.local[colour].wait()
            self.send_second(colour)
            self.send_last(colour, 0, 0)
        elif token[0] == "s":
            colour, s = token[1:]
            for copy in self.flying[token]:
                copy.wait_recv()
            axis = ORDERS[colour][1]
            far, way = SIZES[axis] // 2, 1 if s > 0 else -1
            if self.rings(colour) and s != far:
                half = None if abs(s) < far - 1 else 0 if s < 0 else 1
                part = self.quarter(colour, 0, s, half)
                copy = self.remote(part, part, device_at(moved(self.me, axis, -way)))
                key = ("s", colour, far if half is not None else s + way)
                self.flying.setdefault(key, []).append(copy)
            self.send_last(colour, 0, s)
            if s == far:
                slab = self.tables[colour].at[self.me["core"], self.me[ORDERS[colour][2]]]
                self.handed[token] = [self.remote(slab, slab, self.partner)]
        else:
            colour, k, s = token
            arrived = self.flying[token]
            for copy, _ in arrived:
                copy.wait_recv()
            self.send_last(colour, k + 1, s)
            self.handed[token] = [self.remote(got, got, self.partner) for _, got in arrived]

    def have(self, token):
        for copy in self.handed.pop(token, ()):
            copy.wait_recv()

    def finish(self):
        for copy in self.issued:
            copy.wait_send()


def gather_copies():
    total = 1
    for first, second, last in ORDERS:
        total += SIZES[first] + SIZES[second] + 2 * SIZES[second] * (SIZES[last] - 1)
    return total


def split_two(value):
    high = value.astype(jnp.bfloat16)
    low = (value - high.astype(jnp.float32)).astype(jnp.bfloat16)
    return jnp.concatenate([high, low], axis=0)


def dot(a, b):
    return jnp.dot(a, b, preferred_element_type=jnp.float32)


def groups_of(rows):
    units = units_of(rows)
    return [u // 2 for u in units], units[0] % 2


def codes_of(ids, rows):
    counts, mixed = groups_of(rows)
    bits = rows.bit_length() - 1
    owner, row = ids >> bits, ids & (rows - 1)
    zl, y, x = owner >> 4, (owner >> 2) & 3, owner & 3
    group, r = row >> 4, row & 15
    first = x * (128 * counts[0]) + ((zl * 4 + y) * counts[0] + group) * 16 + r
    at = 512 * counts[0]
    base = counts[0] + mixed
    second = at + y * (128 * counts[1]) + ((zl * 4 + x) * counts[1] + group - base) * 16 + r
    at += 512 * counts[1]
    base += counts[1]
    third = at + (((zl * 4 + y) * 4 + x) * counts[2] + group - base) * 16 + r
    at += 512 * counts[2]
    code = jnp.where(group < base, second, third)
    if mixed:
        shared = at + ((zl * 4 + y) * 4 + x) * 16 + r
        code = jnp.where(group == counts[0], shared, code)
    return jnp.where(group < counts[0], first, code)


def half_step_kernel(n, rows, pack, *refs):
    pieces_ref, ids_ref, conf_ref, mask_ref, start_ref, out_ref = refs[:6]
    packed = refs[6] if pack else None
    scratch = refs[7:] if pack else refs[6:]
    pieces, at = [], 0
    for u in units_of(rows):
        pieces.append(pieces_ref.at[pl.ds(at, u)])
        at += u
    tables = scratch[:3]
    (acc, gram, other, gram2, picked_t, picked, diag, gains, columns, x_s, r_s, p_s) = scratch[3:15]
    gather = Gather(not pack, pieces, tables, *scratch[15:])
    gather.begin()

    counts, mixed = groups_of(rows)
    slots = n * ids_ref.shape[0]

    def along_lanes(ref):
        return jnp.concatenate([ref[k] for k in range(ref.shape[0])], axis=1)

    code = codes_of(along_lanes(ids_ref), rows)
    mask = along_lanes(mask_ref).astype(jnp.float32)
    conf = along_lanes(conf_ref)
    weight, gain = mask * conf, mask * (1.0 + conf)
    total = slots * BLOCKS

    acc[...] = jnp.zeros_like(acc)
    gram[...] = jnp.zeros_like(gram)
    lane = lax.broadcasted_iota(jnp.int32, (n, slots), 1)
    own = lane % n == lax.broadcasted_iota(jnp.int32, (n, slots), 0)
    for g in range(BLOCKS):
        span = slice(g * slots, (g + 1) * slots)
        diag[:, span] = jnp.where(own, weight[g : g + 1, :], 0.0)
        gains[:, span] = split_two(jnp.where(own, gain[g : g + 1, :], 0.0))
        for at in range(0, slots, 128):
            row = jnp.broadcast_to(code[g : g + 1, at : at + 128], (128, 128))
            columns[pl.ds(g * slots + at, 128), :] = row.T

    def add(g, parts, with_gram):
        at = pl.ds(pl.multiple_of(g * slots, 128), slots)
        code = columns[at, :]
        lane = lax.broadcasted_iota(jnp.int32, (slots, 128), 1)
        chosen, held = [], [[], []]
        for tiles, position in parts:
            for first in range(0, 16 * len(tiles), 128):
                hit = lane + (position + first) == code
                chosen.append(jnp.where(hit, 1.0, 0.0).astype(jnp.bfloat16))
            for h in (0, 1):
                held[h] += [t[h] for t in tiles]
        part = jnp.concatenate([jnp.concatenate(t, axis=0) for t in held], axis=1)
        if with_gram:
            gram[...] += dot(part.T, part)
        acc[at, :] += dot(jnp.concatenate(chosen, axis=1), part)

    me = gather.me

    def side_part(g, colour, shift):
        v = moved(me, ORDERS[colour][2], shift)[ORDERS[colour][2]]
        table, count = tables[colour], counts[colour]
        skip = mixed if colour == 1 else 0
        core, z = g % 2, g // 2 * 2
        tiles = [
            [table[(core, v) + ((a, z + zl) if colour else (z + zl, a)) + (skip + 2 * q + h,)] for h in (0, 1)]
            for zl in (0, 1) for a in range(4) for q in range(count)
        ]
        return tiles, 512 * sum(counts[:colour]) + v * (128 * count)

    def shared_part(g):
        core, z = g % 2, g // 2 * 2
        tiles = [
            [tables[0][core, x, z + zl, y, 2 * counts[0]], tables[1][core, y, x, z + zl, 0]]
            for zl in (0, 1) for y in range(NY) for x in range(NX)
        ]
        return tiles, 512 * sum(counts)

    def sides(shifts, pair, last=False):
        for mine in (True, False):
            g = 2 * pair + (me["core"] if mine else 1 - me["core"])
            parts = [side_part(g, colour, s) for colour in (0, 1) for s in shifts]
            add(g, parts + ([shared_part(g)] if last and mixed else []), mine)

    def level(shift):
        v, table, count = moved(me, "z", shift)["z"], tables[2], counts[2]
        for mine in (True, False):
            core = me["core"] if mine else 1 - me["core"]
            tiles = [
                [table[core, v, y, x, 2 * q + h] for h in (0, 1)]
                for y in range(NY) for x in range(NX) for q in range(count)
            ]
            position = 512 * sum(counts[:2]) + v % 2 * (256 * count)
            add(v // 2 * 2 + core, [(tiles, position)], mine)

    def across(pair, _):
        sides((2,), pair, last=True)
        return 0

    def work(what, which):
        last = [parts_of(c)[1] for c in range(3)]
        if what == "own":
            needs, run = [("s", c, last[c]) for c in (0, 1)], lambda: sides((0,), which)
        elif what == "beside":
            needs = [(c, 0, s) for c in (0, 1) for s in parts_of(c)]
            run = lambda: sides((1, -1), which)
        elif what == "across":
            needs = [(c, 1, s) for c in (0, 1) for s in parts_of(c)]
            run = lambda: lax.fori_loop(0, BLOCKS // 2, across, 0)
        else:
            needs = [(2, abs(which) - 1, s) for s in parts_of(2)] if which else [("s", 2, last[2])]
            run = lambda: level(which)
        for need in needs:
            gather.have(need)
        run()

    for token in SCHEDULES[rows] + (("w", "across", 0),):
        if token[0] == "w":
            work(*token[1:])
        else:
            gather.take(token)

    for g in range(BLOCKS):
        span = slice(g * slots, (g + 1) * slots)
        here = acc[span, :]
        picked[span, :] = here.astype(jnp.bfloat16)
        picked_t[:, span] = here.T.astype(jnp.bfloat16)
        if g == 1:
            swap = gather.remote(gram, other, gather.partner)
    rhs = dot(gains[...], picked[...])
    swap.wait_recv()
    whole = gram[...] + other[...]
    high = whole.astype(jnp.bfloat16)
    gram2[:, 0:RANK] = high
    gram2[:, RANK : 2 * RANK] = (whole - high.astype(jnp.float32)).astype(jnp.bfloat16)
    width = 768

    def apply(vector):
        two = split_two(vector)
        by_gram = dot(two, gram2[...])
        image = by_gram[:n, :RANK] + by_gram[:n, RANK:] + by_gram[n:, :RANK] + vector
        extra = jnp.zeros((2 * n, RANK), jnp.float32)
        for at in range(0, total, width):
            along = dot(two, picked_t[:, at : at + width])
            along = (along[:n] + along[n:]) * diag[:, at : at + width]
            extra = extra + dot(split_two(along), picked[at : at + width, :])
        return image + extra[:n] + extra[n:]

    start = start_ref[...]
    resid = rhs[:n] + rhs[n:] - apply(start)
    x_s[...] = start
    r_s[...] = resid
    p_s[...] = resid

    def step(_, now):
        direction = p_s[...]
        image = apply(direction)
        alpha = now / jnp.sum(direction * image, axis=1, keepdims=True)
        x_s[...] += alpha * direction
        left = r_s[...] - alpha * image
        r_s[...] = left
        later = jnp.sum(left * left, axis=1, keepdims=True)
        p_s[...] = left + later / now * direction
        return later

    lax.fori_loop(0, CG_STEPS, step, jnp.sum(resid * resid, axis=1, keepdims=True))
    out = x_s[...]
    out_ref[...] = out
    if pack:
        small = out.astype(jnp.bfloat16)
        for j in range(n // 8):
            packed[j] = small[j // 2 * 16 : j // 2 * 16 + 16, j % 2 * 128 : j % 2 * 128 + 128]
    gather.finish()


def half_step(pieces, slot_arrays, start, rows, pack):
    n, slots = start.shape[0], start.shape[0] * slot_arrays[0].shape[2]
    units = units_of(rows)
    total = BLOCKS * slots
    out_shape = [jax.ShapeDtypeStruct((n, RANK), jnp.float32)]
    if pack:
        out_shape.append(jax.ShapeDtypeStruct((n // 8, 16, 128), jnp.bfloat16))
    near = pl.BlockSpec(memory_space=pltpu.VMEM)
    copies = gather_copies()
    return pl.pallas_call(
        functools.partial(half_step_kernel, n, rows, pack),
        out_shape=out_shape,
        in_specs=[pl.BlockSpec(memory_space=pl.ANY)] + [near] * 4,
        out_specs=[near] * len(out_shape),
        scratch_shapes=[
            *(pltpu.VMEM(buffer_shape(o, u), jnp.bfloat16) for o, u in zip(ORDERS, units)),
            pltpu.VMEM((total, RANK), jnp.float32),
            pltpu.VMEM((RANK, RANK), jnp.float32),
            pltpu.VMEM((RANK, RANK), jnp.float32),
            pltpu.VMEM((RANK, 2 * RANK), jnp.bfloat16),
            pltpu.VMEM((RANK, total), jnp.bfloat16),
            pltpu.VMEM((total, RANK), jnp.bfloat16),
            pltpu.VMEM((n, total), jnp.float32),
            pltpu.VMEM((2 * n, total), jnp.bfloat16),
            pltpu.VMEM((total, 128), jnp.int32),
            pltpu.VMEM((n, RANK), jnp.float32),
            pltpu.VMEM((n, RANK), jnp.float32),
            pltpu.VMEM((n, RANK), jnp.float32),
            pltpu.SemaphoreType.DMA((copies,)),
            pltpu.SemaphoreType.DMA((copies,)),
            pltpu.SemaphoreType.DMA((3,)),
        ],
        compiler_params=pltpu.CompilerParams(
            collective_id=0 if pack else 1, has_side_effects=True, vmem_limit_bytes=60 << 20
        ),
        name=f"half_step_{n}",
    )(pieces, *(a.transpose(2, 1, 0) for a in slot_arrays), start)


def per_device(
    user_factors, item_factors, user_items, user_conf, user_mask, item_users, item_conf, item_mask
):
    users, items = user_factors.shape[0], item_factors.shape[0]
    small = item_factors.astype(jnp.bfloat16).reshape(items // 16, 16, 2, 128)
    small = small.transpose(0, 2, 1, 3).reshape(items // 8, 16, 128)
    new_users, pieces = half_step(small, (user_items, user_conf, user_mask), user_factors, items, True)
    new_items = half_step(pieces, (item_users, item_conf, item_mask), item_factors, users, False)[0]
    return new_users, new_items


def solution(mesh):
    both = ("grp", "dev")
    two, three = P(both, None), P(both, None, None)
    return jax.shard_map(
        per_device,
        mesh=mesh,
        in_specs=(two, two) + (three,) * 6,
        out_specs=(two, two),
        check_vma=False,
    )
```

```python
import functools

import jax
import jax.numpy as jnp
from jax import lax
from jax.experimental import pallas as pl
from jax.experimental.pallas import tpu as pltpu
from jax.sharding import PartitionSpec as P

MESH = pl.DeviceIdType.MESH
CG_STEPS = 4
RANK = 256
NX, NY, NZ = 4, 4, 8
BLOCKS = 8
SIZES = {"x": NX, "y": NY, "z": NZ}
ORDERS = (("y", "z", "x"), ("z", "x", "y"), ("x", "y", "z"))
SCHEDULES = {
    64: (
        ("f", 2), ("f", 0), ("f", 1), ("s", 2, -1), ("s", 2, 1), (2, 0, 0), (0, 0, 0), ("s", 0, -1), ("s", 0, 1), ("s",
        2, 2), ("w", "z", 0), ("s", 1, -1), ("s", 1, 1), (1, 0, 0), (2, 0, -1), (2, 0, 1), (2, 1, 0), ("s", 0, -2),
        ("s", 0, 2), (2, 0, 2), (2, 1, -1), ("s", 1, 2), (0, 1, 0), ("w", "z", 1), (2, 1, 1), (1, 0, -1), (2, 2, 0), (0,
        0, -1), ("w", "z", -1), (0, 0, 1), ("s", 0, -3), ("s", 0, 3), (1, 0, 1), (2, 1, 2), (0, 0, -2), (2, 2, -1), (0,
        0, 2), ("w", "z", 2), (2, 2, 1), (1, 1, 0), (2, 3, 0), ("w", "z", -2), (0, 1, -1), ("s", 0, 4), (1, 0, 2), (0,
        1, 1), (2, 2, 2), (1, 1, -1), (0, 0, -3), ("w", "own", 0), (2, 3, -1), (0, 0, 3), (2, 3, 1), (0, 1, -2), ("w",
        "own", 1), (1, 1, 1), (0, 1, 2), ("w", "own", 2), ("w", "own", 3), (0, 0, 4), (2, 3, 2), ("w", "z", 3), (1, 1,
        2), (0, 1, -3), ("w", "z", -3), (0, 1, 3), ("w", "beside", 0), ("w", "beside", 1), (0, 1, 4), ("w", "beside",
        2), ("w", "beside", 3), ("w", "z", 4)
    ),
    128: (
        ("f", 2), ("f", 0), ("f", 1), ("s", 2, -1), ("s", 2, 1), (2, 0, 0), (0, 0, 0), ("s", 0, -1), ("s", 0, 1), (2, 0,
        -1), (2, 0, 1), ("s", 1, -1), ("s", 1, 1), (1, 0, 0), ("s", 2, 2), (2, 1, 0), (0, 1, 0), ("w", "z", 0), ("s", 0,
        -2), ("s", 0, 2), (0, 0, -1), (2, 1, -1), (2, 1, 1), (0, 0, 1), (2, 0, 2), (1, 0, -1), ("s", 1, 2), (2, 2, 0),
        ("w", "z", 1), ("w", "z", -1), (0, 0, -2), ("s", 0, -3), ("s", 0, 3), (1, 0, 1), (2, 2, -1), (0, 0, 2), (0, 1,
        -1), (2, 2, 1), (2, 1, 2), (0, 1, 1), (1, 1, 0), (1, 1, -1), (0, 1, -2), (2, 3, 0), ("w", "z", 2), ("s", 0, 4),
        (2, 3, -1), ("w", "z", -2), (0, 0, -3), (2, 3, 1), ("w", "own", 0), (2, 2, 2), (1, 0, 2), (0, 0, 3), ("w",
        "own", 1), (0, 1, 2), ("w", "own", 2), ("w", "z", 3), (1, 1, 1), (0, 0, 4), (2, 3, 2), (0, 1, -3), ("w", "own",
        3), ("w", "z", -3), (0, 1, 3), (1, 1, 2), ("w", "beside", 0), (0, 1, 4), ("w", "beside", 1), ("w", "beside", 2),
        ("w", "beside", 3), ("w", "z", 4)
    ),
}


def units_of(rows):
    units = rows // 16 * 2
    last = units // 4
    side = (units - last) // 2
    return (side, side, last)


def buffer_shape(order, units):
    return (2,) + tuple(SIZES[a] for a in order[::-1]) + (units, 16, 128)


def my_coords():
    grp, dev = lax.axis_index("grp"), lax.axis_index("dev")
    core = grp % 2
    z = grp // 2 * 2 + dev // 16
    return {"core": core, "z": z, "y": dev // 4 % 4, "x": dev % 4}


def device_at(coords):
    return {
        "grp": coords["z"] // 2 * 2 + coords["core"],
        "dev": coords["z"] % 2 * 16 + coords["y"] * 4 + coords["x"],
    }


def moved(me, axis, shift):
    size = SIZES[axis]
    return {**me, axis: (me[axis] + shift + size) % size}


def parts_of(colour):
    size = SIZES[ORDERS[colour][1]]
    return (0,) + tuple(shifts_of(size))


def shifts_of(size):
    far = [size // 2]
    return far + [s for d in range(size // 2 - 1, 0, -1) for s in (d, -d)]


class Gather:
    def __init__(self, ring, pieces, tables, send_sem, recv_sem, local_sem):
        self.ring = ring
        self.pieces, self.tables = pieces, tables
        self.send_sem, self.recv_sem, self.local_sem = send_sem, recv_sem, local_sem
        self.me = my_coords()
        self.partner = device_at({**self.me, "core": 1 - self.me["core"]})
        self.issued, self.flying, self.handed, self.local = [], {}, {}, {}

    def greet(self):
        barrier = pltpu.get_barrier_semaphore()
        others = [self.partner]
        for axis, size in SIZES.items():
            others += [device_at(moved(self.me, axis, s)) for s in shifts_of(size)]
        for other in others:
            pl.semaphore_signal(barrier, inc=1, device_id=other, device_id_type=MESH)
        pl.semaphore_wait(barrier, len(others))

    def remote(self, src, dst, target):
        e = len(self.issued)
        copy = pltpu.make_async_remote_copy(
            src_ref=src,
            dst_ref=dst,
            send_sem=self.send_sem.at[e],
            recv_sem=self.recv_sem.at[e],
            device_id=target,
            device_id_type=MESH,
        )
        copy.start()
        self.issued.append(copy)
        return copy

    def send_first(self, colour):
        axis = ORDERS[colour][0]
        dst = self.tables[colour].at[
            (self.me["core"],) + tuple(self.me[a] for a in ORDERS[colour][::-1])
        ]
        self.flying["f", colour] = [
            self.remote(self.pieces[colour], dst, device_at(moved(self.me, axis, s)))
            for s in shifts_of(SIZES[axis])
        ]
        return dst

    def quarter(self, colour, far, s, half=None):
        _, second, last = ORDERS[colour]
        index = (self.me["core"], moved(self.me, last, far)[last], moved(self.me, second, s)[second])
        if half is not None:
            cut = self.tables[colour].shape[3] // 2
            index += (pl.ds(half * cut, cut),)
        return self.tables[colour].at[index]

    def rings(self, colour):
        return self.ring or SIZES[ORDERS[colour][1]] > 4

    def send_second(self, colour):
        axis = ORDERS[colour][1]
        part = self.quarter(colour, 0, 0)
        for s in (1, -1) if self.rings(colour) else (1, -1, 2):
            copy = self.remote(part, part, device_at(moved(self.me, axis, s)))
            self.flying["s", colour, 2 if s == 2 else -s] = [copy]

    def send_last(self, colour, k, s):
        axis = ORDERS[colour][2]
        steps = SIZES[axis] // 2
        if k == steps:
            return
        sent = []
        for way, shift in enumerate((1, -1)):
            if k < steps - 1 or way == s % 2:
                part = self.quarter(colour, -shift * k, s)
                got = self.quarter(colour, -shift * (k + 1), s)
                sent.append((self.remote(part, part, device_at(moved(self.me, axis, shift))), got))
        self.flying[colour, k, s] = sent

    def begin(self):
        self.greet()
        for colour in (2, 0, 1):
            own = self.send_first(colour)
            copy = pltpu.make_async_copy(self.pieces[colour], own, self.local_sem.at[colour])
            copy.start()
            self.local[colour] = copy

    def take(self, token):
        if token[0] == "f":
            colour = token[1]
            for copy in self.flying[token]:
                copy.wait_recv()
            self.local[colour].wait()
            self.send_second(colour)
            self.send_last(colour, 0, 0)
        elif token[0] == "s":
            colour, s = token[1:]
            for copy in self.flying[token]:
                copy.wait_recv()
            axis = ORDERS[colour][1]
            far, way = SIZES[axis] // 2, 1 if s > 0 else -1
            if self.rings(colour) and s != far:
                half = None if abs(s) < far - 1 else 0 if s < 0 else 1
                part = self.quarter(colour, 0, s, half)
                copy = self.remote(part, part, device_at(moved(self.me, axis, -way)))
                key = ("s", colour, far if half is not None else s + way)
                self.flying.setdefault(key, []).append(copy)
            self.send_last(colour, 0, s)
            if s == far:
                slab = self.tables[colour].at[self.me["core"], self.me[ORDERS[colour][2]]]
                self.handed[token] = [self.remote(slab, slab, self.partner)]
        else:
            colour, k, s = token
            arrived = self.flying[token]
            for copy, _ in arrived:
                copy.wait_recv()
            self.send_last(colour, k + 1, s)
            self.handed[token] = [self.remote(got, got, self.partner) for _, got in arrived]

    def have(self, token):
        for copy in self.handed.pop(token, ()):
            copy.wait_recv()

    def finish(self):
        for copy in self.issued:
            copy.wait_send()


def gather_copies():
    total = 1
    for first, second, last in ORDERS:
        total += SIZES[first] + SIZES[second] + 2 * SIZES[second] * (SIZES[last] - 1)
    return total


def split_two(value):
    high = value.astype(jnp.bfloat16)
    low = (value - high.astype(jnp.float32)).astype(jnp.bfloat16)
    return jnp.concatenate([high, low], axis=0)


def dot(a, b):
    return jnp.dot(a, b, preferred_element_type=jnp.float32)


def groups_of(rows):
    units = units_of(rows)
    return [u // 2 for u in units], units[0] % 2


def codes_of(ids, rows):
    counts, mixed = groups_of(rows)
    bits = rows.bit_length() - 1
    owner, row = ids >> bits, ids & (rows - 1)
    zl, y, x = owner >> 4, (owner >> 2) & 3, owner & 3
    group, r = row >> 4, row & 15
    first = x * (128 * counts[0]) + ((zl * 4 + y) * counts[0] + group) * 16 + r
    at = 512 * counts[0]
    base = counts[0] + mixed
    second = at + y * (128 * counts[1]) + ((zl * 4 + x) * counts[1] + group - base) * 16 + r
    at += 512 * counts[1]
    base += counts[1]
    third = at + (((zl * 4 + y) * 4 + x) * counts[2] + group - base) * 16 + r
    at += 512 * counts[2]
    code = jnp.where(group < base, second, third)
    if mixed:
        shared = at + ((zl * 4 + y) * 4 + x) * 16 + r
        code = jnp.where(group == counts[0], shared, code)
    return jnp.where(group < counts[0], first, code)


def half_step_kernel(n, rows, pack, *refs):
    pieces_ref, ids_ref, conf_ref, mask_ref, start_ref, out_ref = refs[:6]
    packed = refs[6] if pack else None
    scratch = refs[7:] if pack else refs[6:]
    pieces, at = [], 0
    for u in units_of(rows):
        pieces.append(pieces_ref.at[pl.ds(at, u)])
        at += u
    tables = scratch[:3]
    (acc, gram, other, gram2, picked_t, picked, diag, gains, columns, x_s, r_s, p_s) = scratch[3:15]
    gather = Gather(not pack, pieces, tables, *scratch[15:])
    gather.begin()

    counts, mixed = groups_of(rows)
    slots = n * ids_ref.shape[0]

    def along_lanes(ref):
        return jnp.concatenate([ref[k] for k in range(ref.shape[0])], axis=1)

    code = codes_of(along_lanes(ids_ref), rows)
    mask = along_lanes(mask_ref).astype(jnp.float32)
    conf = along_lanes(conf_ref)
    weight, gain = mask * conf, mask * (1.0 + conf)
    total = slots * BLOCKS

    acc[...] = jnp.zeros_like(acc)
    gram[...] = jnp.zeros_like(gram)
    lane = lax.broadcasted_iota(jnp.int32, (n, slots), 1)
    own = lane % n == lax.broadcasted_iota(jnp.int32, (n, slots), 0)
    for g in range(BLOCKS):
        span = slice(g * slots, (g + 1) * slots)
        diag[:, span] = jnp.where(own, weight[g : g + 1, :], 0.0)
        gains[:, span] = split_two(jnp.where(own, gain[g : g + 1, :], 0.0))
        for at in range(0, slots, 128):
            row = jnp.broadcast_to(code[g : g + 1, at : at + 128], (128, 128))
            columns[pl.ds(g * slots + at, 128), :] = row.T

    def add(g, parts, with_gram):
        at = pl.ds(pl.multiple_of(g * slots, 128), slots)
        code = columns[at, :]
        lane = lax.broadcasted_iota(jnp.int32, (slots, 128), 1)
        chosen, held = [], [[], []]
        for tiles, position in parts:
            for first in range(0, 16 * len(tiles), 128):
                hit = lane + (position + first) == code
                chosen.append(jnp.where(hit, 1.0, 0.0).astype(jnp.bfloat16))
            for h in (0, 1):
                held[h] += [t[h] for t in tiles]
        part = jnp.concatenate([jnp.concatenate(t, axis=0) for t in held], axis=1)
        if with_gram:
            gram[...] += dot(part.T, part)
        acc[at, :] += dot(jnp.concatenate(chosen, axis=1), part)

    me = gather.me

    def side_part(g, colour, shift):
        v = moved(me, ORDERS[colour][2], shift)[ORDERS[colour][2]]
        table, count = tables[colour], counts[colour]
        skip = mixed if colour == 1 else 0
        core, z = g % 2, g // 2 * 2
        tiles = [
            [table[(core, v) + ((a, z + zl) if colour else (z + zl, a)) + (skip + 2 * q + h,)] for h in (0, 1)]
            for zl in (0, 1) for a in range(4) for q in range(count)
        ]
        return tiles, 512 * sum(counts[:colour]) + v * (128 * count)

    def shared_part(g):
        core, z = g % 2, g // 2 * 2
        tiles = [
            [tables[0][core, x, z + zl, y, 2 * counts[0]], tables[1][core, y, x, z + zl, 0]]
            for zl in (0, 1) for y in range(NY) for x in range(NX)
        ]
        return tiles, 512 * sum(counts)

    def sides(shifts, pair, last=False):
        for mine in (True, False):
            g = 2 * pair + (me["core"] if mine else 1 - me["core"])
            parts = [side_part(g, colour, s) for colour in (0, 1) for s in shifts]
            add(g, parts + ([shared_part(g)] if last and mixed else []), mine)

    def level(shift):
        v, table, count = moved(me, "z", shift)["z"], tables[2], counts[2]
        for mine in (True, False):
            core = me["core"] if mine else 1 - me["core"]
            tiles = [
                [table[core, v, y, x, 2 * q + h] for h in (0, 1)]
                for y in range(NY) for x in range(NX) for q in range(count)
            ]
            position = 512 * sum(counts[:2]) + v % 2 * (256 * count)
            add(v // 2 * 2 + core, [(tiles, position)], mine)

    def across(pair, _):
        sides((2,), pair, last=True)
        return 0

    def work(what, which):
        last = [parts_of(c)[1] for c in range(3)]
        if what == "own":
            needs, run = [("s", c, last[c]) for c in (0, 1)], lambda: sides((0,), which)
        elif what == "beside":
            needs = [(c, 0, s) for c in (0, 1) for s in parts_of(c)]
            run = lambda: sides((1, -1), which)
        elif what == "across":
            needs = [(c, 1, s) for c in (0, 1) for s in parts_of(c)]
            run = lambda: lax.fori_loop(0, BLOCKS // 2, across, 0)
        else:
            needs = [(2, abs(which) - 1, s) for s in parts_of(2)] if which else [("s", 2, last[2])]
            run = lambda: level(which)
        for need in needs:
            gather.have(need)
        run()

    for token in SCHEDULES[rows] + (("w", "across", 0),):
        if token[0] == "w":
            work(*token[1:])
        else:
            gather.take(token)

    for g in range(BLOCKS):
        span = slice(g * slots, (g + 1) * slots)
        here = acc[span, :].astype(jnp.bfloat16)
        picked[span, :] = here
        picked_t[:, span] = here.T
        if g == 1:
            swap = gather.remote(gram, other, gather.partner)
    rhs = dot(gains[...], picked[...])
    swap.wait_recv()
    whole = gram[...] + other[...]
    high = whole.astype(jnp.bfloat16)
    gram2[:, 0:RANK] = high
    gram2[:, RANK : 2 * RANK] = (whole - high.astype(jnp.float32)).astype(jnp.bfloat16)
    width = 768

    def apply(vector):
        two = split_two(vector)
        by_gram = dot(two, gram2[...])
        image = by_gram[:n, :RANK] + by_gram[:n, RANK:] + by_gram[n:, :RANK] + vector
        extra = jnp.zeros((2 * n, RANK), jnp.float32)
        for at in range(0, total, width):
            along = dot(two, picked_t[:, at : at + width])
            along = (along[:n] + along[n:]) * diag[:, at : at + width]
            extra = extra + dot(split_two(along), picked[at : at + width, :])
        return image + extra[:n] + extra[n:]

    start = start_ref[...]
    resid = rhs[:n] + rhs[n:] - apply(start)
    x_s[...] = start
    r_s[...] = resid
    p_s[...] = resid

    def step(_, now):
        direction = p_s[...]
        image = apply(direction)
        alpha = now / jnp.sum(direction * image, axis=1, keepdims=True)
        x_s[...] += alpha * direction
        left = r_s[...] - alpha * image
        r_s[...] = left
        later = jnp.sum(left * left, axis=1, keepdims=True)
        p_s[...] = left + later / now * direction
        return later

    lax.fori_loop(0, CG_STEPS, step, jnp.sum(resid * resid, axis=1, keepdims=True))
    out = x_s[...]
    out_ref[...] = out
    if pack:
        small = out.astype(jnp.bfloat16)
        for j in range(n // 8):
            packed[j] = small[j // 2 * 16 : j // 2 * 16 + 16, j % 2 * 128 : j % 2 * 128 + 128]
    gather.finish()


def half_step(pieces, slot_arrays, start, rows, pack):
    n, slots = start.shape[0], start.shape[0] * slot_arrays[0].shape[2]
    units = units_of(rows)
    total = BLOCKS * slots
    out_shape = [jax.ShapeDtypeStruct((n, RANK), jnp.float32)]
    if pack:
        out_shape.append(jax.ShapeDtypeStruct((n // 8, 16, 128), jnp.bfloat16))
    near = pl.BlockSpec(memory_space=pltpu.VMEM)
    copies = gather_copies()
    return pl.pallas_call(
        functools.partial(half_step_kernel, n, rows, pack),
        out_shape=out_shape,
        in_specs=[pl.BlockSpec(memory_space=pl.ANY)] + [near] * 4,
        out_specs=[near] * len(out_shape),
        scratch_shapes=[
            *(pltpu.VMEM(buffer_shape(o, u), jnp.bfloat16) for o, u in zip(ORDERS, units)),
            pltpu.VMEM((total, RANK), jnp.float32),
            pltpu.VMEM((RANK, RANK), jnp.float32),
            pltpu.VMEM((RANK, RANK), jnp.float32),
            pltpu.VMEM((RANK, 2 * RANK), jnp.bfloat16),
            pltpu.VMEM((RANK, total), jnp.bfloat16),
            pltpu.VMEM((total, RANK), jnp.bfloat16),
            pltpu.VMEM((n, total), jnp.float32),
            pltpu.VMEM((2 * n, total), jnp.bfloat16),
            pltpu.VMEM((total, 128), jnp.int32),
            pltpu.VMEM((n, RANK), jnp.float32),
            pltpu.VMEM((n, RANK), jnp.float32),
            pltpu.VMEM((n, RANK), jnp.float32),
            pltpu.SemaphoreType.DMA((copies,)),
            pltpu.SemaphoreType.DMA((copies,)),
            pltpu.SemaphoreType.DMA((3,)),
        ],
        compiler_params=pltpu.CompilerParams(
            collective_id=0 if pack else 1, has_side_effects=True, vmem_limit_bytes=60 << 20
        ),
        name=f"half_step_{n}",
    )(pieces, *(a.transpose(2, 1, 0) for a in slot_arrays), start)


def per_device(
    user_factors, item_factors, user_items, user_conf, user_mask, item_users, item_conf, item_mask
):
    users, items = user_factors.shape[0], item_factors.shape[0]
    small = item_factors.astype(jnp.bfloat16).reshape(items // 16, 16, 2, 128)
    small = small.transpose(0, 2, 1, 3).reshape(items // 8, 16, 128)
    new_users, pieces = half_step(small, (user_items, user_conf, user_mask), user_factors, items, True)
    new_items = half_step(pieces, (item_users, item_conf, item_mask), item_factors, users, False)[0]
    return new_users, new_items


def solution(mesh):
    both = ("grp", "dev")
    two, three = P(both, None), P(both, None, None)
    return jax.shard_map(
        per_device,
        mesh=mesh,
        in_specs=(two, two) + (three,) * 6,
        out_specs=(two, two),
        check_vma=False,
    )
```
